128 devices in a mesh: ta: 8 (over y_lo, x), gz: 8 (over z, core), col: 2 (over y_hi).
Axes of the slice: x: 4, y: 4 (y_hi: 2, y_lo: 2; y = y_hi * 2 + y_lo), z: 4, core: 2. Of those that a mesh axis runs over, the one named last changes fastest.
Arguments:
- rhs_field: float32 [1, 96, 64, 32, 128], P(None, None, ('ta', 'col'), 'gz'), may hold values from -6 to 6
- link_weights: float32 [8, 64, 32, 128], P(None, ('ta', 'col'), 'gz'), may hold values from 0.4 to 1.6
- fine_blocks: float32 [9, 96, 96], replicated, may hold values from -1 to 5
- smoother: float32 [96, 96], replicated, may hold values from -1 to 1
- plane_next: int32 [4, 128], replicated, may hold values from 0 to 127, as said below
- aggregate: int32 [128], replicated, may hold values from 0 to 7, as said below
- restrict_map: float32 [96, 128], replicated, may hold values from -0.625 to 0.625
- prolong_map: float32 [128, 96], replicated, may hold values from -0.5 to 0.5
- coarse_blocks: float32 [9, 128, 128], replicated, may hold values from -1 to 5
- coarse_smoother: float32 [128, 128], replicated, may hold values from -1 to 1
- coarse_next: int32 [4, 8], replicated, may hold values from 0 to 7, as said below
Outputs:
- solution: float32 [1, 96, 64, 32, 128], P(None, None, ('ta', 'col'), 'gz')
- residual: float32 [1, 96, 64, 32, 128], P(None, None, ('ta', 'col'), 'gz')
The draws below stay inside these ranges and needn't reach their ends.
Inputs may be any that keep to these rules, and one draw needn't show every extreme that they name: `plane_next`: each row is an ordering of the plane sites; row 1 undoes row 0 and row 3 undoes row 2. `aggregate`: each coarse plane site is named by exactly 16 entries. `coarse_next`: each row is an ordering of the coarse plane sites; row 1 undoes row 0 and row 3 undoes row 2.
All inputs are finite; a program needn't handle non-finite values.
Results may differ from the reference program's by a relative error of at most 0.0003.
Values sent between devices are 32-bit elements; how exact they have to be, the bound alone decides.
No kernel may reach another device: no remote copies, remote signals or barrier semaphores. Data moves between devices by JAX's collectives and lax.ppermute only.
A program may use at most 64 MiB of HBM per device.

```python
import math
import jax
import jax.numpy as jnp
from jax import lax

CF = 96
CC = 128
RHS = 1
PLANE = 128
AGG = 16
SWEEPS = 3
NT = 64
NZ = 32
CPLANE = 8


def noise_draw(key, shape):
    return jnp.clip(jax.random.normal(key, shape, jnp.float32), -5.0, 5.0)


def block_set(key, order):
    first, second = jax.random.split(key)
    center = 4.0 * jnp.eye(order, dtype=jnp.float32) + noise_draw(first, (order, order)) / jnp.sqrt(jnp.float32(order))
    hops = 0.25 * noise_draw(second, (8, order, order)) / jnp.sqrt(jnp.float32(order))
    return jnp.concatenate([center[None], hops], axis=0)


def smoother_draw(key, order):
    return 0.25 * jnp.eye(order, dtype=jnp.float32) + 0.06 * noise_draw(key, (order, order)) / jnp.sqrt(jnp.float32(order))


def neighbour_table(key, count):
    first, second = jax.random.split(key)
    forward_x = jax.random.permutation(first, count).astype(jnp.int32)
    forward_y = jax.random.permutation(second, count).astype(jnp.int32)
    back_x = jnp.argsort(forward_x).astype(jnp.int32)
    back_y = jnp.argsort(forward_y).astype(jnp.int32)
    return jnp.stack([forward_x, back_x, forward_y, back_y]).astype(jnp.int32)


def draw_fine_blocks(key, part):
    return block_set(jax.random.fold_in(key, 11), CF)


def draw_smoother(key, part):
    return smoother_draw(jax.random.fold_in(key, 12), CF)


def draw_coarse_blocks(key, part):
    return block_set(jax.random.fold_in(key, 13), CC)


def draw_coarse_smoother(key, part):
    return smoother_draw(jax.random.fold_in(key, 14), CC)


def draw_plane_next(key, part):
    return neighbour_table(jax.random.fold_in(key, 15), PLANE)


def draw_coarse_next(key, part):
    return neighbour_table(jax.random.fold_in(key, 16), CPLANE)


def draw_aggregate(key, part):
    order = jax.random.permutation(jax.random.fold_in(key, 17), PLANE).astype(jnp.int32)
    return (order // AGG).astype(jnp.int32)


def block_levels(stream_key, shape, cuts, least, high):
    def one(position, parts):
        draws = jax.random.uniform(jax.random.fold_in(jax.random.fold_in(stream_key, 6), position), (parts,), jnp.float32, least / len(cuts), high / len(cuts))
        return jnp.repeat(jnp.exp(draws), shape[position] // parts).reshape((-1,) + (1,) * (len(shape) - position - 1))

    factor_of = one(*cuts[0])
    for cut in cuts[1:]:
        factor_of = factor_of * one(*cut)
    return factor_of


def gaussian(rng, dims, spread, most, cuts=(), kind=jnp.bfloat16):
    factor_of = block_levels(rng, dims, cuts, -0.22, 0.18) if cuts else 1.0
    array = jax.random.normal(rng, dims, jnp.float32) * spread * factor_of
    return jnp.minimum(jnp.maximum(array, -most), most).astype(kind)


def setup_inputs(seed: int = 0) -> dict:
    splits = jax.random.split(jax.random.key(seed), 12)
    return {
        "rhs_field": gaussian(splits[0], (RHS, CF, NT, NZ, PLANE), 1.0, 6.0, ((2, 16), (3, 8)), jnp.float32),
        "link_weights": jnp.clip(jnp.exp(math.log(1.6) - 1.3862944 * jax.random.uniform(splits[1], (8, NT, NZ, PLANE), jnp.float32) ** block_levels(splits[1], (8, NT, NZ, PLANE), ((1, 16), (2, 8)), -0.2, 0.2)), 0.4, 1.6),
        "fine_blocks": draw_fine_blocks(jax.random.fold_in(splits[11], 71), 0),
        "smoother": draw_smoother(jax.random.fold_in(splits[11], 71), 0),
        "plane_next": draw_plane_next(jax.random.fold_in(splits[11], 71), 0),
        "aggregate": draw_aggregate(jax.random.fold_in(splits[11], 71), 0),
        "restrict_map": gaussian(splits[6], (CF, CC), CF ** -0.5, 0.625, (), jnp.float32),
        "prolong_map": gaussian(splits[7], (CC, CF), CC ** -0.5, 0.5, (), jnp.float32),
        "coarse_blocks": draw_coarse_blocks(jax.random.fold_in(splits[11], 71), 0),
        "coarse_smoother": draw_coarse_smoother(jax.random.fold_in(splits[11], 71), 0),
        "coarse_next": draw_coarse_next(jax.random.fold_in(splits[11], 71), 0),
    }


def block_fine(matrix, field):
    return jnp.einsum("ij,rjtzp->ritzp", matrix, field, precision=lax.Precision.HIGHEST)


def block_coarse(matrix, field):
    return jnp.einsum("ij,rtzqj->rtzqi", matrix, field, precision=lax.Precision.HIGHEST)


def reference(rhs_field, link_weights, fine_blocks, smoother, plane_next, aggregate, restrict_map, prolong_map, coarse_blocks, coarse_smoother, coarse_next):
    onehot = (aggregate[:, None] == jnp.arange(CPLANE, dtype=jnp.int32)[None, :]).astype(jnp.float32)

    def fine_apply(field):
        padded = jnp.pad(field, ((0, 0), (0, 0), (1, 1), (1, 1), (0, 0)), mode="wrap")
        output = block_fine(fine_blocks[0], field)
        for direction in range(8):
            if direction == 0:
                neighbour = padded[:, :, 2:, 1:-1]
            elif direction == 1:
                neighbour = padded[:, :, :-2, 1:-1]
            elif direction == 2:
                neighbour = padded[:, :, 1:-1, 2:]
            elif direction == 3:
                neighbour = padded[:, :, 1:-1, :-2]
            else:
                neighbour = jnp.take(field, plane_next[direction - 4], axis=4)
            output = output + link_weights[direction][None, None] * block_fine(fine_blocks[direction + 1], neighbour)
        return output

    def coarse_apply(field):
        padded = jnp.pad(field, ((0, 0), (1, 1), (1, 1), (0, 0), (0, 0)), mode="wrap")
        output = block_coarse(coarse_blocks[0], field)
        for direction in range(8):
            if direction == 0:
                neighbour = padded[:, 2:, 1:-1]
            elif direction == 1:
                neighbour = padded[:, :-2, 1:-1]
            elif direction == 2:
                neighbour = padded[:, 1:-1, 2:]
            elif direction == 3:
                neighbour = padded[:, 1:-1, :-2]
            else:
                neighbour = jnp.take(field, coarse_next[direction - 4], axis=3)
            output = output + block_coarse(coarse_blocks[direction + 1], neighbour)
        return output

    solution = block_fine(smoother, rhs_field)
    solution = solution + block_fine(smoother, rhs_field - fine_apply(solution))
    fine_residual = rhs_field - fine_apply(solution)
    summed = jnp.einsum("rctzp,pq->rctzq", fine_residual, onehot, precision=lax.Precision.HIGHEST)
    coarse_rhs = jnp.einsum("rctzq,ck->rtzqk", summed, restrict_map, precision=lax.Precision.HIGHEST)
    values = block_coarse(coarse_smoother, coarse_rhs)
    for sweep_index in range(SWEEPS):
        values = values + block_coarse(coarse_smoother, coarse_rhs - coarse_apply(values))
    lifted = jnp.einsum("rtzqk,kc->rctzq", values, prolong_map, precision=lax.Precision.HIGHEST)
    solution = solution + jnp.einsum("rctzq,pq->rctzp", lifted, onehot, precision=lax.Precision.HIGHEST)
    for sweep_index in range(2):
        solution = solution + block_fine(smoother, rhs_field - fine_apply(solution))
    residual = rhs_field - fine_apply(solution)
    return solution, residual
```

```python
import functools

import jax
import jax.numpy as jnp
from jax import lax
from jax.experimental import pallas as pl
from jax.experimental.pallas import tpu as pltpu
from jax.sharding import PartitionSpec as P

F32, BF16 = jnp.float32, jnp.bfloat16
CF, CC, PL, NB, CP = 96, 128, 128, 9, 8
KF, KC = NB * CF, NB * CC
SWEEPS = 3
TAXES = ("ta", "col")


def halves(value):
    high = value.astype(BF16)
    return high, (value - high.astype(F32)).astype(BF16)


def dot(left, right):
    return jnp.dot(left, right, preferred_element_type=F32)


def dot_nt(left, right):
    return lax.dot_general(left, right, (((1,), (1,)), ((), ())), preferred_element_type=F32)


def lanes_of(value, index):
    return jnp.take_along_axis(value, index, axis=1)


def stack_matrix(source, target):
    high, low = halves(source[...])
    target[0:CF, :] = high
    target[CF : 2 * CF, :] = low


def product(matrix, high, low):
    both = dot(matrix[...], high[...])
    return both[0:CF] + both[CF : 2 * CF] + dot(matrix[0:CF, :], low[...])


def put(high, low, row, column, value):
    top, rest = halves(value)
    rows, columns = pl.ds(row, CF), pl.ds(column * PL, PL)
    high[rows, columns] = top
    low[rows, columns] = rest


def fill(field, site, stride, weights, plane, high, low, column):
    here = field[site]
    put(high, low, 0, column, here)
    for hop, offset in enumerate((stride, -stride, 1, -1)):
        put(high, low, (hop + 1) * CF, column, field[site + offset] * weights[hop : hop + 1])
    for hop in range(4):
        there = lanes_of(here, plane[hop]) * weights[hop + 4 : hop + 5]
        put(high, low, (hop + 5) * CF, column, there)


def ring_pair(index):
    inside = index < 12
    side = index - 12
    t = jnp.where(inside, lax.div(index, 3), jnp.where(side < 2, -1, 4))
    z = jnp.where(inside, 2 * lax.rem(index, 3) - 1, 2 * lax.rem(side + 2, 2))
    return t, z


def block_pair(index):
    return lax.div(index, 2), 2 * lax.rem(index, 2)


def grid6(t, z):
    return (t + 1) * 6 + z + 1


def grid8(t, z):
    return (t + 2) * 8 + z + 2


def each(count, step):
    def body(index, carry):
        step(2 * index, 0)
        step(2 * index + 1, 1)
        return carry

    lax.fori_loop(0, count // 2, body, 0)


def plane_tables(ref):
    return [jnp.broadcast_to(ref[hop : hop + 1, :], (CF, PL)) for hop in range(4)]


def pre_kernel(
    u, htm, htp, hzm, hzp, ctm, ctp, s_ref, m_ref, b_ref, r_ref, plane_ref, member_ref,
    x1_out, x0_out, lw_out, crhs_out,
    smat, mmat, bmat, x0, lw, high, low, vhigh, vlow, summed,
):
    stack_matrix(s_ref, smat)
    stack_matrix(m_ref, mmat)
    stack_matrix(b_ref, bmat)
    plane = plane_tables(plane_ref)

    def smooth(slot, source, first, second, target, other):
        for column, site in ((0, first), (1, second)):
            put(high.at[slot], low.at[slot], 0, column, source[site, 0:CF, :])
        value = product(smat, high.at[slot, 0:CF], low.at[slot, 0:CF])
        x0[target] = value[:, 0:PL]
        x0[other] = value[:, PL : 2 * PL]
        lw[target] = source[first, CF : CF + 8, :]
        lw[other] = source[second, CF : CF + 8, :]

    def rows_of(source, base_t):
        def step(index, slot):
            t, z = block_pair(index)
            place = grid8(t + base_t, z)
            smooth(slot, source, 2 * index, 2 * index + 1, place, place + 1)

        return step

    def columns_of(source, base_z):
        def step(index, slot):
            place = grid8(index, base_z)
            smooth(slot, source, 2 * index, 2 * index + 1, place, place + 1)

        return step

    each(8, rows_of(u, 0))
    each(4, rows_of(htm, -2))
    each(4, rows_of(htp, 4))
    each(4, columns_of(hzm, -2))
    each(4, columns_of(hzp, 4))
    smooth(0, ctm, 0, 1, grid8(-1, -1), grid8(-1, 4))
    smooth(1, ctp, 0, 1, grid8(4, -1), grid8(4, 4))

    def sweep(index, slot):
        t, z = ring_pair(index)
        place, out = grid8(t, z), grid6(t, z)
        for column in range(2):
            fill(x0, place + column, 8, lw[place + column], plane, vhigh.at[slot], vlow.at[slot], column)
        value = product(mmat, vhigh.at[slot], vlow.at[slot])
        for column in range(2):
            old = x0[place + column]
            x0_out[out + column] = old
            lw_out[out + column] = lw[place + column]
            x1_out[out + column] = 2.0 * old - value[:, column * PL : (column + 1) * PL]

    each(16, sweep)

    member = member_ref[...].astype(BF16)

    def left_over(index, slot):
        t, z = block_pair(index)
        place = grid6(t, z)
        for column in range(2):
            fill(x1_out, place + column, 6, lw_out[place + column], plane, vhigh.at[slot], vlow.at[slot], column)
        value = product(bmat, vhigh.at[slot], vlow.at[slot])
        for column in range(2):
            rest = u[2 * index + column, 0:CF, :] - value[:, column * PL : (column + 1) * PL]
            top, tail = halves(rest)
            total = dot_nt(member, top) + dot_nt(member, tail)
            summed[pl.ds((2 * index + column) * 8, 8), :] = total[0:8]

    each(8, left_over)
    top, tail = halves(summed[...])
    rtop, rtail = halves(r_ref[...])
    crhs = dot(top, rtop) + dot(tail, rtop) + dot(top, rtail)
    crhs_out[...] = crhs.reshape(16, CP, CC)


def mid_kernel(
    c, zcm, zcp, tcm, tcp, cs_ref, cm_ref, plane_ref, coarse_ref, prolong_ref, lift_ref,
    x1, x0, lw, m_ref,
    x3_out,
    mmat, cmat, w0, w, chigh, clow, lifted, field, vhigh, vlow,
):
    stack_matrix(m_ref, mmat)
    plane = plane_tables(plane_ref)
    cmat[:, 0:CC], cmat[:, CC : 2 * CC] = halves(cm_ref[...])

    for t in range(4):
        w[pl.ds((t + 4) * 12, 4)] = zcm[4 * t : 4 * t + 4]
        w[pl.ds((t + 4) * 12 + 4, 4)] = c[4 * t : 4 * t + 4]
        w[pl.ds((t + 4) * 12 + 8, 4)] = zcp[4 * t : 4 * t + 4]
        for base, source in ((0, tcm), (8, tcp)):
            w[(t + base) * 12] = jnp.zeros((CP, CC), F32)
            w[pl.ds((t + base) * 12 + 1, 10)] = source[10 * t : 10 * t + 10]
            w[(t + base) * 12 + 11] = jnp.zeros((CP, CC), F32)
    top, tail = halves(w[...].reshape(144 * CP, CC))
    ctop, ctail = halves(cs_ref[...])
    first = (dot(top, ctop) + dot(tail, ctop) + dot(top, ctail)).reshape(144, CP, CC)
    w0[...] = first
    w[...] = first
    turn = [coarse_ref[hop] for hop in range(4)]

    for sweep in range(SWEEPS):
        side = 10 - 2 * sweep
        corner = (1 + sweep) * 13
        rows = side * CP

        def gather_row(t, carry, side=side, corner=corner, rows=rows):
            start = corner + t * 12
            place = pl.ds(pl.multiple_of(t * rows, 16), rows)
            for hop, offset in enumerate((0, 12, -12, 1, -1)):
                block = w[pl.ds(start + offset, side)].reshape(rows, CC)
                top, tail = halves(block)
                chigh[place, hop * CC : (hop + 1) * CC] = top
                clow[place, hop * CC : (hop + 1) * CC] = tail
            for hop in range(4):
                block = jnp.concatenate(
                    [jnp.take_along_axis(w[start + z], turn[hop], axis=0) for z in range(side)], axis=0
                )
                top, tail = halves(block)
                chigh[place, (hop + 5) * CC : (hop + 6) * CC] = top
                clow[place, (hop + 5) * CC : (hop + 6) * CC] = tail
            return carry

        lax.fori_loop(0, side, gather_row, 0)
        total = side * rows
        both = dot(chigh[0:total, :], cmat[...])
        change = both[:, 0:CC] + both[:, CC : 2 * CC] + dot(clow[0:total, :], cmat[:, 0:CC])
        for t in range(side):
            start = corner + t * 12
            old = w[pl.ds(start, side)] + w0[pl.ds(start, side)]
            w[pl.ds(start, side)] = old - change[t * rows : (t + 1) * rows].reshape(side, CP, CC)

    near = jnp.concatenate([w[pl.ds((t + 3) * 12 + 3, 6)] for t in range(6)], axis=0)
    near = jnp.concatenate([near.reshape(36 * CP, CC), jnp.zeros((12 * CP, CC), F32)], axis=0)
    top, tail = halves(near)
    ptop, ptail = halves(prolong_ref[...])
    up = dot_nt(ptop, top) + dot_nt(ptop, tail) + dot_nt(ptail, top)
    for part in range(3):
        lifted[part] = up[:, part * PL : (part + 1) * PL]
    home = jnp.broadcast_to(lift_ref[0:1, :], (CF, PL))

    def correct(index, slot):
        t, z = ring_pair(index)
        for column in range(2):
            place = grid6(t, z) + column
            part, spot = lax.div(place, 16), lax.rem(place, 16)
            field[place] = x1[place] + lanes_of(lifted[part], home + CP * spot)

    each(16, correct)

    def sweep_fine(index, slot):
        t, z = block_pair(index)
        place = grid6(t, z)
        for column in range(2):
            fill(field, place + column, 6, lw[place + column], plane, vhigh.at[slot], vlow.at[slot], column)
        value = product(mmat, vhigh.at[slot], vlow.at[slot])
        for column in range(2):
            old = field[place + column] + x0[place + column]
            x3_out[2 * index + column] = old - value[:, column * PL : (column + 1) * PL]

    each(8, sweep_fine)


def post_kernel(
    x3, htm, htp, hzm, hzp, ctm, ctp, u, x0, lw, m_ref, b_ref, plane_ref,
    sol_out, res_out,
    mmat, bmat, wide, field, vhigh, vlow,
):
    stack_matrix(m_ref, mmat)
    stack_matrix(b_ref, bmat)
    plane = plane_tables(plane_ref)
    for t in range(4):
        wide[pl.ds(grid8(t, 0), 4)] = x3[4 * t : 4 * t + 4]
        wide[pl.ds(grid8(t, -2), 2)] = hzm[2 * t : 2 * t + 2]
        wide[pl.ds(grid8(t, 4), 2)] = hzp[2 * t : 2 * t + 2]
    for t in range(2):
        wide[pl.ds(grid8(t - 2, 0), 4)] = htm[4 * t : 4 * t + 4]
        wide[pl.ds(grid8(t + 4, 0), 4)] = htp[4 * t : 4 * t + 4]
    for side in range(2):
        wide[grid8(-1, -1 + 5 * side)] = ctm[side]
        wide[grid8(4, -1 + 5 * side)] = ctp[side]

    def sweep(index, slot):
        t, z = ring_pair(index)
        place, out = grid8(t, z), grid6(t, z)
        for column in range(2):
            fill(wide, place + column, 8, lw[out + column], plane, vhigh.at[slot], vlow.at[slot], column)
        value = product(mmat, vhigh.at[slot], vlow.at[slot])
        for column in range(2):
            old = wide[place + column] + x0[out + column]
            field[out + column] = old - value[:, column * PL : (column + 1) * PL]

    each(16, sweep)

    def left_over(index, slot):
        t, z = block_pair(index)
        place = grid6(t, z)
        for column in range(2):
            fill(field, place + column, 6, lw[place + column], plane, vhigh.at[slot], vlow.at[slot], column)
        value = product(bmat, vhigh.at[slot], vlow.at[slot])
        for column in range(2):
            sol_out[2 * index + column] = field[place + column]
            rest = u[2 * index + column, 0:CF, :] - value[:, column * PL : (column + 1) * PL]
            res_out[2 * index + column] = rest

    each(8, left_over)


def call(kernel, outs, scratch, name):
    vmem = pl.BlockSpec(memory_space=pltpu.VMEM)
    shapes = tuple(jax.ShapeDtypeStruct(shape, F32) for shape in outs)
    return lambda *args: pl.pallas_call(
        kernel,
        out_shape=shapes,
        in_specs=[vmem] * len(args),
        out_specs=tuple(vmem for _ in outs),
        scratch_shapes=[pltpu.VMEM(shape, kind) for shape, kind in scratch],
        compiler_params=pltpu.CompilerParams(vmem_limit_bytes=48 << 20),
        name=name,
    )(*args)


def moved(value, axes, step):
    count = 1
    for axis in axes if isinstance(axes, tuple) else (axes,):
        count *= lax.axis_size(axis)
    return lax.ppermute(value, axes, [(i, (i + step) % count) for i in range(count)])


def fine_halo(value):
    rows = value.shape[2:]
    zm = moved(value[:, 2:4], "gz", 1)
    zp = moved(value[:, 0:2], "gz", -1)
    tm = moved(value[2:4], TAXES, 1)
    tp = moved(value[0:2], TAXES, -1)
    ctm = moved(jnp.stack([zm[3, 1], zp[3, 0]]), TAXES, 1)
    ctp = moved(jnp.stack([zm[0, 1], zp[0, 0]]), TAXES, -1)
    flat = [part.reshape((8,) + rows) for part in (tm, tp, zm, zp)]
    return (*flat, ctm, ctp)


def shards(
    rhs_field,
    link_weights,
    fine_blocks,
    smoother,
    plane_next,
    aggregate,
    restrict_map,
    prolong_map,
    coarse_blocks,
    coarse_smoother,
    coarse_next,
):
    exact = functools.partial(jnp.einsum, precision=lax.Precision.HIGHEST)
    rhs = jnp.transpose(rhs_field[0], (1, 2, 0, 3))
    weights = jnp.transpose(link_weights, (1, 2, 0, 3))
    packed = jnp.concatenate([rhs, weights], axis=2)
    u = packed.reshape(16, CF + 8, PL)
    halo = fine_halo(packed)

    bmat = jnp.transpose(fine_blocks, (1, 0, 2)).reshape(CF, KF)
    mmat = exact("im,mk->ik", smoother, bmat)
    cmat = exact("kmj,im->kji", coarse_blocks, coarse_smoother).reshape(KC, CC)
    member = (jnp.arange(16, dtype=jnp.int32)[:, None] == aggregate[None, :]).astype(F32)
    turn = jnp.broadcast_to(coarse_next[:, :, None], (4, CP, CC))
    home = jnp.broadcast_to(aggregate[None, :], (8, PL))

    grid = ((36, CF, PL), (36, CF, PL), (36, 8, PL), (16, CP, CC))
    stacked = ((2, KF, 2 * PL), BF16)
    x1, x0, lw, crhs = call(
        pre_kernel,
        grid,
        (
            ((2 * CF, CF), BF16),
            ((2 * CF, KF), BF16),
            ((2 * CF, KF), BF16),
            ((64, CF, PL), F32),
            ((64, 8, PL), F32),
            ((2, CF, 2 * PL), BF16),
            ((2, CF, 2 * PL), BF16),
            stacked,
            stacked,
            ((16 * CP, CF), F32),
        ),
        "pre",
    )(u, *halo, smoother, mmat, bmat, restrict_map, plane_next, member)

    c = crhs.reshape(4, 4, CP, CC)
    zcm = moved(c, "gz", 1)
    zcp = moved(c, "gz", -1)
    broad = jnp.concatenate([zcm[:, 1:4], c, zcp[:, 0:3]], axis=1)
    tcm = moved(broad, TAXES, 1)
    tcp = moved(broad, TAXES, -1)

    (x3,) = call(
        mid_kernel,
        ((16, CF, PL),),
        (
            ((2 * CF, KF), BF16),
            ((KC, 2 * CC), BF16),
            ((144, CP, CC), F32),
            ((144, CP, CC), F32),
            ((800, KC), BF16),
            ((800, KC), BF16),
            ((3, CF, PL), F32),
            ((36, CF, PL), F32),
            stacked,
            stacked,
        ),
        "mid",
    )(
        crhs,
        zcm.reshape(16, CP, CC),
        zcp.reshape(16, CP, CC),
        tcm.reshape(40, CP, CC),
        tcp.reshape(40, CP, CC),
        coarse_smoother.T,
        cmat,
        plane_next,
        turn,
        prolong_map.T,
        home,
        x1,
        x0,
        lw,
        mmat,
    )

    sol, res = call(
        post_kernel,
        ((16, CF, PL), (16, CF, PL)),
        (
            ((2 * CF, KF), BF16),
            ((2 * CF, KF), BF16),
            ((64, CF, PL), F32),
            ((36, CF, PL), F32),
            stacked,
            stacked,
        ),
        "post",
    )(x3, *fine_halo(x3.reshape(4, 4, CF, PL)), u, x0, lw, mmat, bmat, plane_next)

    def natural(value):
        return jnp.transpose(value.reshape(4, 4, CF, PL), (2, 0, 1, 3))[None]

    return natural(sol), natural(res)


def solution(mesh):
    spread = P(None, None, TAXES, "gz", None)
    return jax.shard_map(
        shards,
        mesh=mesh,
        in_specs=(spread, P(None, TAXES, "gz", None)) + (P(),) * 9,
        out_specs=(spread, spread),
        check_vma=False,
    )
```

```python
import jax
import jax.numpy as jnp
from jax import lax
from jax.experimental import pallas as pl
from jax.experimental.pallas import tpu as pltpu
from jax.sharding import PartitionSpec as P

F32, BF16 = jnp.float32, jnp.bfloat16
CF, CC, PL, NB, CP = 96, 128, 128, 9, 8
KF, KC = NB * CF, NB * CC
SWEEPS = 3
TAXES = ("ta", "col")


def halves(value):
    high = value.astype(BF16)
    return high, (value - high.astype(F32)).astype(BF16)


def dot(left, right):
    return jnp.dot(left, right, preferred_element_type=F32)


def dot_nt(left, right):
    return lax.dot_general(left, right, (((1,), (1,)), ((), ())), preferred_element_type=F32)


def lanes_of(value, index):
    return jnp.take_along_axis(value, index, axis=1)


def product(matrix, high, low):
    both = dot(matrix[...], high[...])
    return both[0:CF] + both[CF : 2 * CF] + dot(matrix[0:CF, :], low[...])


def put(high, low, row, column, value):
    top, rest = halves(value)
    rows, columns = pl.ds(row, CF), pl.ds(column * PL, PL)
    high[rows, columns] = top
    low[rows, columns] = rest


def fill(field, site, stride, weights, plane, high, low, column):
    here = field[site]
    put(high, low, 0, column, here)
    for hop, offset in enumerate((stride, -stride, 1, -1)):
        put(high, low, (hop + 1) * CF, column, field[site + offset] * weights[hop : hop + 1])
    for hop in range(4):
        there = lanes_of(here, plane[hop]) * weights[hop + 4 : hop + 5]
        put(high, low, (hop + 5) * CF, column, there)


def place(t, z):
    return (t + 2) * 8 + z + 2


def middle_pair(index):
    return 1 + lax.div(index, 3), 2 * lax.rem(index, 3) - 1


def outer_pair(index):
    wide = index < 6
    side = index - 6
    t = jnp.where(wide, 3 * lax.div(index, 3), jnp.where(side < 2, -1, 4))
    z = jnp.where(wide, 2 * lax.rem(index, 3) - 1, 2 * lax.rem(side + 6, 2))
    return t, z


def ring_pair(index):
    inside = index < 12
    side = index - 12
    t = jnp.where(inside, lax.div(index, 3), jnp.where(side < 2, -1, 4))
    z = jnp.where(inside, 2 * lax.rem(index, 3) - 1, 2 * lax.rem(side + 12, 2))
    return t, z


def each(count, load, finish):
    load(0, 0)

    def body(index, carry):
        load(2 * index + 1, 1)
        finish(2 * index, 0)
        load(2 * index + 2, 0)
        finish(2 * index + 1, 1)
        return carry

    lax.fori_loop(0, count // 2 - 1, body, 0)
    load(count - 1, 1)
    finish(count - 2, 0)
    finish(count - 1, 1)


def plane_tables(ref):
    return [jnp.broadcast_to(ref[hop : hop + 1, :], (CF, PL)) for hop in range(4)]


def smooth(smat, high, low, x0, sources, targets):
    for column, source in enumerate(sources):
        put(high, low, 0, column, source)
    value = product(smat, high.at[0:CF], low.at[0:CF])
    for column, target in enumerate(targets):
        x0[target] = value[:, column * PL : (column + 1) * PL]


def sweeps(count, where, matrix, field, x0, lw, plane, vhigh, vlow, target):
    def load(index, slot):
        site = place(*where(index))
        for column in range(2):
            fill(field, site + column, 8, lw[site + column], plane, vhigh.at[slot], vlow.at[slot], column)

    def finish(index, slot):
        site = place(*where(index))
        change = product(matrix, vhigh.at[slot], vlow.at[slot])
        for column in range(2):
            old = field[site + column] + x0[site + column]
            target[site + column] = old - change[:, column * PL : (column + 1) * PL]

    each(count, load, finish)


def block_pairs(matrix, field, lw, plane, vhigh, vlow, finish):
    def load(index):
        site, slot = place(index // 2, 2 * (index % 2)), index % 2
        for column in range(2):
            fill(field, site + column, 8, lw[site + column], plane, vhigh.at[slot], vlow.at[slot], column)

    load(0)
    for index in range(8):
        if index < 7:
            load(index + 1)
        slot = index % 2
        image = product(matrix, vhigh.at[slot], vlow.at[slot])
        finish(index // 2, slot, [image[:, 0:PL], image[:, PL : 2 * PL]])


def exact_dot(left, right):
    parts = []
    for value in (left, right):
        top, rest = halves(value)
        tail = (value - top.astype(F32) - rest.astype(F32)).astype(BF16)
        parts.append((top, rest, tail))
    (l0, l1, l2), (r0, r1, r2) = parts
    small = dot(l0, r2) + dot(l1, r1) + dot(l2, r0)
    return small + (dot(l0, r1) + dot(l1, r0)) + dot(l0, r0)


def prepare_kernel(s_ref, blocks, cs_ref, coarse, smat, mmat, bmat, cmat):
    smooth_matrix = s_ref[...]
    smat[0:CF, :], smat[CF : 2 * CF, :] = halves(smooth_matrix)
    whole = jnp.concatenate([blocks[k] for k in range(NB)], axis=1)
    bmat[0:CF, :], bmat[CF : 2 * CF, :] = halves(whole)
    mmat[0:CF, :], mmat[CF : 2 * CF, :] = halves(exact_dot(smooth_matrix, whole))
    coarse_smooth = cs_ref[...]
    for k in range(NB):
        turned = jnp.transpose(exact_dot(coarse_smooth, coarse[k]), (1, 0))
        rows = slice(k * CC, (k + 1) * CC)
        cmat[rows, 0:CC], cmat[rows, CC : 2 * CC] = halves(turned)


def local_kernel(
    a0, a1, a2, a3, l_ref, hzm, hzp, smat, mmat, plane_ref,
    x0, lw, x1,
    vhigh, vlow,
):
    plane = plane_tables(plane_ref)
    for t, row in enumerate((a0, a1, a2, a3)):
        for pair in range(2):
            site = place(t, 2 * pair)
            slot = pair
            smooth(smat, vhigh.at[slot], vlow.at[slot], x0, [row[2 * pair], row[2 * pair + 1]], [site, site + 1])
        for z in range(4):
            lw[place(t, z)] = l_ref[:, 4 * t + z, :]
        for slot, (source, z) in enumerate(((hzm, -2), (hzp, 4))):
            site = place(t, z)
            smooth(
                smat, vhigh.at[slot], vlow.at[slot], x0,
                [source[2 * t, 0:CF, :], source[2 * t + 1, 0:CF, :]], [site, site + 1],
            )
        lw[place(t, -1)] = hzm[2 * t + 1, CF : CF + 8, :]
        lw[place(t, 4)] = hzp[2 * t, CF : CF + 8, :]

    sweeps(6, middle_pair, mmat, x0, x0, lw, plane, vhigh, vlow, x1)


def pre_kernel(
    a0, a1, a2, a3, tm1, tm2, tp1, tp2, czm, czp, smat, mmat, bmat, r_ref, plane_ref, member_ref,
    x0_in, lw_in, x1_in,
    x0, lw, x1, crhs_out,
    vhigh, vlow, summed,
):
    plane = plane_tables(plane_ref)
    for near, far, t_near, t_far in ((tm1, tm2, -1, -2), (tp1, tp2, 4, 5)):
        for pair in range(2):
            for slot, (source, t) in enumerate(((near, t_near), (far, t_far))):
                site = place(t, 2 * pair)
                smooth(
                    smat, vhigh.at[slot], vlow.at[slot], x0,
                    [source[2 * pair, 0:CF, :], source[2 * pair + 1, 0:CF, :]], [site, site + 1],
                )
        lw[pl.ds(place(t_near, 0), 4)] = near[:, CF : CF + 8, :]
    for slot, (source, z) in enumerate(((czm, -1), (czp, 4))):
        smooth(
            smat, vhigh.at[slot], vlow.at[slot], x0,
            [source[0], source[1]], [place(-1, z), place(4, z)],
        )

    sweeps(10, outer_pair, mmat, x0, x0, lw, plane, vhigh, vlow, x1)

    member = member_ref[...].astype(BF16)
    rows = (a0, a1, a2, a3)

    def finish(t, half, images):
        for column, image in enumerate(images):
            top, tail = halves(rows[t][2 * half + column] - image)
            total = dot_nt(member, top) + dot_nt(member, tail)
            number = 4 * t + 2 * half + column
            summed[number * 8 : number * 8 + 8, :] = total[0:8]

    block_pairs(bmat, x1, lw, plane, vhigh, vlow, finish)
    top, tail = halves(summed[...])
    rtop, rtail = halves(r_ref[...])
    crhs = dot(top, rtop) + dot(tail, rtop) + dot(top, rtail)
    crhs_out[...] = crhs.reshape(16, CP, CC)


def mid_kernel(
    c, tcm, tcp, zcm, zcp, cs_ref, cmat, plane_ref, coarse_ref, prolong_ref, lift_ref,
    x1, x0, lw, mmat,
    wide, r0, r1, r2, r3, zlow, zhigh,
    w0, w, chigh, clow, lifted, field, vhigh, vlow,
):
    plane = plane_tables(plane_ref)
    blank = jnp.zeros((4, CP, CC), F32)
    for t in range(12):
        source, row = ((tcm, t), (c, t - 4), (tcp, t - 8))[t // 4]
        w[pl.ds(t * 12 + 4, 4)] = source[4 * row : 4 * row + 4]
        side = t - 1
        known = 0 <= side < 10
        w[pl.ds(t * 12, 4)] = zcm[4 * side : 4 * side + 4] if known else blank
        w[pl.ds(t * 12 + 8, 4)] = zcp[4 * side : 4 * side + 4] if known else blank
    top, tail = halves(w[...].reshape(144 * CP, CC))
    ctop, ctail = halves(cs_ref[...])
    first = (dot_nt(top, ctop) + dot_nt(tail, ctop) + dot_nt(top, ctail)).reshape(144, CP, CC)
    w0[...] = first
    w[...] = first
    turn = [coarse_ref[hop] for hop in range(4)]

    for sweep in range(SWEEPS):
        side = 10 - 2 * sweep
        corner = (1 + sweep) * 13
        rows = side * CP

        def gather_row(t, carry, side=side, corner=corner, rows=rows):
            start = corner + t * 12
            place = pl.ds(pl.multiple_of(t * rows, 16), rows)
            for hop, offset in enumerate((0, 12, -12, 1, -1)):
                block = w[pl.ds(start + offset, side)].reshape(rows, CC)
                top, tail = halves(block)
                chigh[place, hop * CC : (hop + 1) * CC] = top
                clow[place, hop * CC : (hop + 1) * CC] = tail
            for hop in range(4):
                block = jnp.concatenate(
                    [jnp.take_along_axis(w[start + z], turn[hop], axis=0) for z in range(side)], axis=0
                )
                top, tail = halves(block)
                chigh[place, (hop + 5) * CC : (hop + 6) * CC] = top
                clow[place, (hop + 5) * CC : (hop + 6) * CC] = tail
            return carry

        lax.fori_loop(0, side, gather_row, 0)
        total = side * rows
        both = dot(chigh[0:total, :], cmat[...])
        change = both[:, 0:CC] + both[:, CC : 2 * CC] + dot(clow[0:total, :], cmat[:, 0:CC])
        for t in range(side):
            start = corner + t * 12
            old = w[pl.ds(start, side)] + w0[pl.ds(start, side)]
            w[pl.ds(start, side)] = old - change[t * rows : (t + 1) * rows].reshape(side, CP, CC)

    near = jnp.concatenate([w[pl.ds((t + 3) * 12 + 3, 6)] for t in range(6)], axis=0)
    near = jnp.concatenate([near.reshape(36 * CP, CC), jnp.zeros((12 * CP, CC), F32)], axis=0)
    top, tail = halves(near)
    ptop, ptail = halves(prolong_ref[...])
    up = dot_nt(ptop, top) + dot_nt(ptop, tail) + dot_nt(ptail, top)
    for part in range(3):
        lifted[part] = up[:, part * PL : (part + 1) * PL]
    home = jnp.broadcast_to(lift_ref[0:1, :], (CF, PL))

    def correct(index, carry):
        t, z = ring_pair(index)
        for column in range(2):
            number = (t + 1) * 6 + z + 1 + column
            part, spot = lax.div(number, 16), lax.rem(number, 16)
            site = place(t, z) + column
            field[site] = x1[site] + lanes_of(lifted[part], home + CP * spot)
        return carry

    lax.fori_loop(0, 16, correct, 0)
    rows, half_of = (r0, r1, r2, r3), (zlow, zhigh)

    def finish(t, half, changes):
        for column, change in enumerate(changes):
            site = place(t, 2 * half + column)
            new = field[site] + x0[site] - change
            wide[site] = new
            rows[t][2 * half + column] = new
            half_of[half][2 * t + column] = new

    block_pairs(mmat, field, lw, plane, vhigh, vlow, finish)


def inner_kernel(wide_in, hzm, hzp, x0, lw, mmat, plane_ref, wide, x4, vhigh, vlow):
    plane = plane_tables(plane_ref)
    for t in range(4):
        wide[pl.ds(place(t, -2), 2)] = hzm[2 * t : 2 * t + 2]
        wide[pl.ds(place(t, 4), 2)] = hzp[2 * t : 2 * t + 2]

    sweeps(6, middle_pair, mmat, wide, x0, lw, plane, vhigh, vlow, x4)


def post_kernel(
    wide_in, x4_in, tm1, tm2, tp1, tp2, czm, czp, a0, a1, a2, a3, x0, lw, mmat, bmat, plane_ref,
    wide, x4, sol_out, res_out,
    vhigh, vlow, rest, sems,
):
    plane = plane_tables(plane_ref)
    for source, t in ((tm1, -1), (tm2, -2), (tp1, 4), (tp2, 5)):
        wide[pl.ds(place(t, 0), 4)] = source[...]
    for source, z in ((czm, -1), (czp, 4)):
        wide[place(-1, z)] = source[0]
        wide[place(4, z)] = source[1]

    sweeps(10, outer_pair, mmat, wide, x0, lw, plane, vhigh, vlow, x4)

    def send(source, target, number, kind):
        copy = pltpu.make_async_copy(source, target.at[:, number, :], sems.at[kind, number])
        copy.start()
        return copy

    copies = [send(x4.at[place(n // 4, n % 4)], sol_out, n, 0) for n in range(16)]
    rows = (a0, a1, a2, a3)

    def finish(t, half, images):
        for column, image in enumerate(images):
            number = 4 * t + 2 * half + column
            rest[number] = rows[t][2 * half + column] - image
            copies.append(send(rest.at[number], res_out, number, 1))

    block_pairs(bmat, x4, lw, plane, vhigh, vlow, finish)
    for copy in copies:
        copy.wait()


STACKED = ((2, KF, 2 * PL), BF16)
FRAME = ((64, CF, PL), F32)
WEIGHTS = ((64, 8, PL), F32)
ROW = ((4, CF, PL), F32)
PAIRED = ((2 * CF, KF), BF16)


def call(name, kernel, outs, scratch, aliases, *args, limit=8, far=()):
    vmem, away = pl.BlockSpec(memory_space=pltpu.VMEM), pl.BlockSpec(memory_space=pl.ANY)
    return pl.pallas_call(
        kernel,
        out_shape=tuple(jax.ShapeDtypeStruct(shape, kind) for shape, kind in outs),
        in_specs=[vmem] * len(args),
        out_specs=tuple(away if number in far else vmem for number in range(len(outs))),
        scratch_shapes=[
            pltpu.VMEM(*entry) if isinstance(entry, tuple) else entry for entry in scratch
        ],
        input_output_aliases=aliases,
        compiler_params=pltpu.CompilerParams(vmem_limit_bytes=limit << 20),
        name=name,
    )(*args)


def moved(value, axes, step):
    count = 1
    for axis in axes if isinstance(axes, tuple) else (axes,):
        count *= lax.axis_size(axis)
    return lax.ppermute(value, axes, [(i, (i + step) % count) for i in range(count)])


def fine_halo(r0, r1, r2, r3, zlow, zhigh):
    tm1, tp1 = moved(r3, TAXES, 1), moved(r0, TAXES, -1)
    tm2, tp2 = moved(r2, TAXES, 1), moved(r1, TAXES, -1)
    hzm, hzp = moved(zhigh, "gz", 1), moved(zlow, "gz", -1)
    czm = moved(jnp.stack([tm1[3, 0:CF], tp1[3, 0:CF]]), "gz", 1)
    czp = moved(jnp.stack([tm1[0, 0:CF], tp1[0, 0:CF]]), "gz", -1)
    return (tm1, tm2, tp1, tp2, czm, czp), (hzm, hzp)


def shards(
    rhs_field,
    link_weights,
    fine_blocks,
    smoother,
    plane_next,
    aggregate,
    restrict_map,
    prolong_map,
    coarse_blocks,
    coarse_smoother,
    coarse_next,
):
    rows = [jnp.transpose(rhs_field[0, :, t], (1, 0, 2)) for t in range(4)]
    lows, highs = (
        jnp.concatenate(
            [
                jnp.transpose(rhs_field[0, :, :, z : z + 2], (1, 2, 0, 3)),
                jnp.transpose(link_weights[:, :, z : z + 2], (1, 2, 0, 3)),
            ],
            axis=2,
        ).reshape(8, CF + 8, PL)
        for z in (0, 2)
    )
    ends = [
        jnp.concatenate([rows[t], jnp.transpose(link_weights[:, t], (1, 0, 2))], axis=1) for t in (0, 3)
    ]
    t_halo, z_halo = fine_halo(ends[0], rows[1], rows[2], ends[1], lows, highs)

    smat, mpair, bpair, cpair = call(
        "prepare",
        prepare_kernel,
        (((2 * CF, CF), BF16), PAIRED, PAIRED, ((KC, 2 * CC), BF16)),
        (),
        {},
        smoother, fine_blocks, coarse_smoother, coarse_blocks,
    )
    member = (jnp.arange(16, dtype=jnp.int32)[:, None] == aggregate[None, :]).astype(F32)
    turn = jnp.broadcast_to(coarse_next[:, :, None], (4, CP, CC))
    home = jnp.broadcast_to(aggregate[None, :], (8, PL))

    x0, lw, x1 = call(
        "local",
        local_kernel,
        (FRAME, WEIGHTS, FRAME),
        (STACKED, STACKED),
        {},
        *rows, link_weights.reshape(8, 16, PL), *z_halo, smat, mpair, plane_next,
    )
    x0, lw, x1, crhs = call(
        "pre",
        pre_kernel,
        (FRAME, WEIGHTS, FRAME, ((16, CP, CC), F32)),
        (STACKED, STACKED, ((16 * CP, CF), F32)),
        {16: 0, 17: 1, 18: 2},
        *rows, *t_halo, smat, mpair, bpair, restrict_map, plane_next, member, x0, lw, x1,
    )

    tcm = moved(crhs, TAXES, 1)
    tcp = moved(crhs, TAXES, -1)
    tall = jnp.concatenate([tcm[4:16], crhs, tcp[0:12]], axis=0)
    zcm = moved(tall, "gz", 1)
    zcp = moved(tall, "gz", -1)

    wide, *parts = call(
        "mid",
        mid_kernel,
        (FRAME, ROW, ROW, ROW, ROW, ((8, CF, PL), F32), ((8, CF, PL), F32)),
        (
            ((144, CP, CC), F32),
            ((144, CP, CC), F32),
            ((800, KC), BF16),
            ((800, KC), BF16),
            ((3, CF, PL), F32),
            FRAME,
            STACKED,
            STACKED,
        ),
        {},
        crhs, tcm, tcp, zcm, zcp, coarse_smoother, cpair, plane_next, turn, prolong_map.T, home,
        x1, x0, lw, mpair,
        limit=16,
    )
    t_halo, z_halo = fine_halo(*parts)
    wide, x4 = call(
        "inner",
        inner_kernel,
        (FRAME, FRAME),
        (STACKED, STACKED),
        {0: 0},
        wide, *z_halo, x0, lw, mpair, plane_next,
    )
    _, _, sol, res = call(
        "post",
        post_kernel,
        (FRAME, FRAME, ((CF, 16, PL), F32), ((CF, 16, PL), F32)),
        (STACKED, STACKED, ((16, CF, PL), F32), pltpu.SemaphoreType.DMA((2, 16))),
        {0: 0, 1: 1},
        wide, x4, *t_halo, *rows, x0, lw, mpair, bpair, plane_next,
        far=(2, 3),
    )

    def natural(value):
        return value.reshape(1, CF, 4, 4, PL)

    return natural(sol), natural(res)


def solution(mesh):
    spread = P(None, None, TAXES, "gz", None)
    return jax.shard_map(
        shards,
        mesh=mesh,
        in_specs=(spread, P(None, TAXES, "gz", None)) + (P(),) * 9,
        out_specs=(spread, spread),
        check_vma=False,
    )
```

```python
import jax
import jax.numpy as jnp
from jax import lax
from jax.experimental import pallas as pl
from jax.experimental.pallas import tpu as pltpu
from jax.sharding import PartitionSpec as P


F32, BF16 = jnp.float32, jnp.bfloat16
CF, CC, PL, NB, CP = 96, 128, 128, 9, 8
KF, KC = NB * CF, NB * CC
SWEEPS = 3
TAXES = ("ta", "col")


def halves(value):
    high = value.astype(BF16)
    return high, (value - high.astype(F32)).astype(BF16)


def dot(left, right):
    return jnp.dot(left, right, preferred_element_type=F32)


def dot_nt(left, right):
    return lax.dot_general(left, right, (((1,), (1,)), ((), ())), preferred_element_type=F32)


def lanes_of(value, index):
    return jnp.take_along_axis(value, index, axis=1)


def product(matrix, high, low):
    both = dot(matrix[...], high[...])
    return both[0:CF] + both[CF : 2 * CF] + dot(matrix[0:CF, :], low[...])


def put(high, low, row, column, value):
    top, rest = halves(value)
    rows, columns = pl.ds(row, CF), pl.ds(column * PL, PL)
    high[rows, columns] = top
    low[rows, columns] = rest


def fill(field, site, stride, weights, plane, high, low, column):
    here = field[site]
    put(high, low, 0, column, here)
    for hop, offset in enumerate((stride, -stride, 1, -1)):
        put(high, low, (hop + 1) * CF, column, field[site + offset] * weights[hop : hop + 1])
    for hop in range(4):
        there = lanes_of(here, plane[hop]) * weights[hop + 4 : hop + 5]
        put(high, low, (hop + 5) * CF, column, there)


def place(t, z):
    return (t + 2) * 8 + z + 2


def middle_pair(index):
    return 1 + lax.div(index, 3), 2 * lax.rem(index, 3) - 1


def edge_pair(index):
    return 3 * lax.div(index, 3), 2 * lax.rem(index, 3) - 1


def outer_pair(index):
    return 5 * lax.div(index, 2) - 1, 2 * lax.rem(index, 2)


def each(count, load, finish):
    load(0, 0)

    def body(index, carry):
        load(2 * index + 1, 1)
        finish(2 * index, 0)
        load(2 * index + 2, 0)
        finish(2 * index + 1, 1)
        return carry

    lax.fori_loop(0, count // 2 - 1, body, 0)
    load(count - 1, 1)
    finish(count - 2, 0)
    finish(count - 1, 1)


def plane_tables(ref):
    return [jnp.broadcast_to(ref[hop : hop + 1, :], (CF, PL)) for hop in range(4)]


def smooth(smat, high, low, x0, sources, targets):
    for column, source in enumerate(sources):
        put(high, low, 0, column, source)
    value = product(smat, high.at[0:CF], low.at[0:CF])
    for column, target in enumerate(targets):
        x0[target] = value[:, column * PL : (column + 1) * PL]


def sweeps(count, where, matrix, field, x0, lw, plane, vhigh, vlow, target):
    def load(index, slot):
        site = place(*where(index))
        for column in range(2):
            fill(field, site + column, 8, lw[site + column], plane, vhigh.at[slot], vlow.at[slot], column)

    def finish(index, slot):
        site = place(*where(index))
        change = product(matrix, vhigh.at[slot], vlow.at[slot])
        for column in range(2):
            old = field[site + column] + x0[site + column]
            target[site + column] = old - change[:, column * PL : (column + 1) * PL]

    each(count, load, finish)


def block_pairs(rows, matrix, field, lw, plane, vhigh, vlow, finish):
    pairs = [(t, half) for t in rows for half in range(2)]

    def load(t, half):
        site = place(t, 2 * half)
        for column in range(2):
            fill(field, site + column, 8, lw[site + column], plane, vhigh.at[half], vlow.at[half], column)

    load(*pairs[0])
    for number, (t, half) in enumerate(pairs):
        if number + 1 < len(pairs):
            load(*pairs[number + 1])
        image = product(matrix, vhigh.at[half], vlow.at[half])
        finish(t, half, [image[:, 0:PL], image[:, PL : 2 * PL]])


def blank_rows(field, first, count):
    for t in (-1, 4):
        field[pl.ds(place(t, first), count)] = jnp.zeros((count, CF, PL), F32)


def one_hop(matrix, values, vhigh, vlow, slot):
    for column, value in enumerate(values):
        put(vhigh.at[slot], vlow.at[slot], 0, column, value)
    image = product(matrix, vhigh.at[slot, 0:CF], vlow.at[slot, 0:CF])
    return [image[:, 0:PL], image[:, PL : 2 * PL]]


def close_edges(hops, field, lw, vhigh, vlow, target):
    for number, (t, outside, hop) in enumerate(((3, 4, 0), (0, -1, 1))):
        for pair in range(3):
            z = 2 * pair - 1
            here, there = place(t, z), place(outside, z)
            values = [field[there + c] * lw[here + c, hop : hop + 1, :] for c in range(2)]
            changes = one_hop(hops.at[hop], values, vhigh, vlow, (number + pair) % 2)
            for c in range(2):
                target[here + c] = target[here + c] - changes[c]


def exact_dot(left, right):
    parts = []
    for value in (left, right):
        top, rest = halves(value)
        tail = (value - top.astype(F32) - rest.astype(F32)).astype(BF16)
        parts.append((top, rest, tail))
    (l0, l1, l2), (r0, r1, r2) = parts
    small = dot(l0, r2) + dot(l1, r1) + dot(l2, r0)
    return small + (dot(l0, r1) + dot(l1, r0)) + dot(l0, r0)


def pair_matrix(target, row, depth, value):
    high, low = halves(value)
    target[row : row + CC, 0:CC] = high
    target[row : row + CC, CC : 2 * CC] = low
    target[depth + row : depth + row + CC, 0:CC] = high
    target[depth + row : depth + row + CC, CC : 2 * CC] = jnp.zeros((CC, CC), BF16)


def prepare_kernel(s_ref, blocks, cs_ref, coarse, smat, mmat, bmat, cmat, csmat, mhops, bhops):
    smooth_matrix = s_ref[...]
    smat[0:CF, :], smat[CF : 2 * CF, :] = halves(smooth_matrix)
    whole = jnp.concatenate([blocks[k] for k in range(NB)], axis=1)
    bmat[0:CF, :], bmat[CF : 2 * CF, :] = halves(whole)
    mmat[0:CF, :], mmat[CF : 2 * CF, :] = halves(exact_dot(smooth_matrix, whole))
    for hop in range(2):
        block = blocks[hop + 1]
        bhops[hop, 0:CF, :], bhops[hop, CF : 2 * CF, :] = halves(block)
        mhops[hop, 0:CF, :], mhops[hop, CF : 2 * CF, :] = halves(exact_dot(smooth_matrix, block))
    coarse_smooth = cs_ref[...]
    for k in range(NB):
        pair_matrix(cmat, k * CC, KC, jnp.transpose(exact_dot(coarse_smooth, coarse[k]), (1, 0)))
    pair_matrix(csmat, 0, CC, jnp.transpose(coarse_smooth, (1, 0)))


def local_kernel(
    a0, a1, a2, a3, l_ref, hzm, hzp, smat, mmat, plane_ref,
    x0, lw, x1,
    vhigh, vlow,
):
    plane = plane_tables(plane_ref)
    for t, row in enumerate((a0, a1, a2, a3)):
        for pair in range(2):
            site = place(t, 2 * pair)
            slot = pair
            smooth(smat, vhigh.at[slot], vlow.at[slot], x0, [row[2 * pair], row[2 * pair + 1]], [site, site + 1])
        for z in range(4):
            lw[place(t, z)] = l_ref[:, 4 * t + z, :]
        for slot, (source, z) in enumerate(((hzm, -2), (hzp, 4))):
            site = place(t, z)
            smooth(
                smat, vhigh.at[slot], vlow.at[slot], x0,
                [source[2 * t, 0:CF, :], source[2 * t + 1, 0:CF, :]], [site, site + 1],
            )
        lw[place(t, -1)] = hzm[2 * t + 1, CF : CF + 8, :]
        lw[place(t, 4)] = hzp[2 * t, CF : CF + 8, :]

    blank_rows(x0, -1, 6)
    blank_rows(x1, 0, 4)
    sweeps(6, middle_pair, mmat, x0, x0, lw, plane, vhigh, vlow, x1)


def edge_kernel(x0, lw, x1_in, mmat, plane_ref, x1, vhigh, vlow):
    plane = plane_tables(plane_ref)
    sweeps(6, edge_pair, mmat, x0, x0, lw, plane, vhigh, vlow, x1)


def pre_kernel(
    a0, a1, a2, a3, tm1, tp1, ctm, ctp, smat, bmat, mhops, bhops, r_ref, plane_ref, member_ref,
    x0_in, lw_in, x1_in,
    x0, lw, x1, up_out, down_out, first_out, last_out,
    vhigh, vlow, summed,
):
    plane = plane_tables(plane_ref)
    for source, t in ((tm1, -1), (tp1, 4)):
        for slot in range(2):
            site = place(t, 2 * slot)
            smooth(
                smat, vhigh.at[slot], vlow.at[slot], x0,
                [source[2 * slot, 0:CF, :], source[2 * slot + 1, 0:CF, :]], [site, site + 1],
            )
        lw[pl.ds(place(t, 0), 4)] = source[:, CF : CF + 8, :]
    for slot, (source, t) in enumerate(((ctm, -1), (ctp, 4))):
        smooth(
            smat, vhigh.at[slot], vlow.at[slot], x0,
            [source[0], source[1]], [place(t, -1), place(t, 4)],
        )

    close_edges(mhops, x0, lw, vhigh, vlow, x1)
    first_out[...] = x1[pl.ds(place(0, 0), 4)]
    last_out[...] = x1[pl.ds(place(3, 0), 4)]

    member = member_ref[...].astype(BF16)
    rows = (a0, a1, a2, a3)

    def restrict(number, value):
        top, tail = halves(value)
        total = dot_nt(member, top) + dot_nt(member, tail)
        summed[number * 8 : number * 8 + 8, :] = total[0:8]

    def finish(t, half, images):
        for column, image in enumerate(images):
            restrict(4 * t + 2 * half + column, rows[t][2 * half + column] - image)

    block_pairs(range(4), bmat, x1, lw, plane, vhigh, vlow, finish)
    for base, t, outside, hop in ((16, 3, 4, 1), (20, 0, -1, 0)):
        for half in range(2):
            here, there = place(t, 2 * half), place(outside, 2 * half)
            values = [x1[here + c] * lw[there + c, hop : hop + 1, :] for c in range(2)]
            images = one_hop(bhops.at[hop], values, vhigh, vlow, half)
            for c in range(2):
                restrict(base + 2 * half + c, -images[c])
    top, tail = halves(summed[...])
    rtop, rtail = halves(r_ref[...])
    crhs = dot(top, rtop) + dot(tail, rtop) + dot(top, rtail)
    crhs = crhs.reshape(24, CP, CC)
    up_out[...] = crhs[0:20]
    down_out[0:16] = crhs[0:16]
    down_out[16:20] = crhs[20:24]


def join_kernel(up, down, tcm, tcp, whole, tall):
    whole[0:16] = tcm[0:16]
    whole[12:16] = tcm[12:16] + down[16:20]
    whole[16:32] = up[0:16]
    whole[16:20] = up[0:4] + tcm[16:20]
    whole[28:32] = up[12:16] + tcp[16:20]
    whole[32:48] = tcp[0:16]
    whole[32:36] = tcp[0:4] + up[16:20]
    tall[...] = whole[4:44]


def diamond(radius):
    rows = []
    for t in range(-radius, 4 + radius):
        reach = radius - max(0, -t, t - 3)
        rows.append((t, -reach, 4 + 2 * reach))
    return rows


def coarse_kernel(
    whole, e2m, e2p, zcm, zcp, csmat, cmat, coarse_ref, prolong_ref,
    lifted,
    w0, w, packed, operand,
):
    for t in range(12):
        own = whole[4 * t : 4 * t + 4]
        if t in (0, 11):
            own = own + (e2p if t else e2m)[...]
        w[pl.ds(t * 12 + 4, 4)] = own
        side = t - 1
        if 0 <= side < 10:
            w[pl.ds(t * 12, 4)] = zcm[4 * side : 4 * side + 4]
            w[pl.ds(t * 12 + 8, 4)] = zcp[4 * side : 4 * side + 4]

    def spot(t, z):
        return (t + 4) * 12 + z + 4

    row = 0
    for t, z, count in diamond(4):
        size = count * CP
        top, tail = halves(w[pl.ds(spot(t, z), count)].reshape(size, CC))
        packed[row : row + size, 0:CC] = top
        packed[row : row + size, CC : 2 * CC] = tail
        row += size
    both = dot(packed[...], csmat[...])
    first = both[:, 0:CC] + both[:, CC : 2 * CC]
    row = 0
    for t, z, count in diamond(4):
        size = count * CP
        value = first[row : row + size].reshape(count, CP, CC)
        w0[pl.ds(spot(t, z), count)] = value
        w[pl.ds(spot(t, z), count)] = value
        row += size
    turn = [coarse_ref[hop] for hop in range(4)]

    for sweep in range(SWEEPS):
        shape = diamond(SWEEPS - sweep)
        row = 0
        for t, z, count in shape:
            size = count * CP
            start = spot(t, z)
            blocks = [w[pl.ds(start + offset, count)].reshape(size, CC) for offset in (0, 12, -12, 1, -1)]
            for hop in range(4):
                blocks.append(
                    jnp.concatenate(
                        [jnp.take_along_axis(w[start + n], turn[hop], axis=0) for n in range(count)], axis=0
                    )
                )
            for hop, block in enumerate(blocks):
                top, tail = halves(block)
                operand[row : row + size, hop * CC : (hop + 1) * CC] = top
                operand[row : row + size, KC + hop * CC : KC + (hop + 1) * CC] = tail
            row += size
        both = dot(operand[0:row, :], cmat[...])
        change = both[:, 0:CC] + both[:, CC : 2 * CC]
        row = 0
        for t, z, count in shape:
            size = count * CP
            place_of = pl.ds(spot(t, z), count)
            w[place_of] = w[place_of] + w0[place_of] - change[row : row + size].reshape(count, CP, CC)
            row += size

    near = jnp.concatenate([w[pl.ds(spot(t, -1), 6)] for t in range(-1, 5)], axis=0)
    near = jnp.concatenate([near.reshape(36 * CP, CC), jnp.zeros((12 * CP, CC), F32)], axis=0)
    top, tail = halves(near)
    ptop, ptail = halves(prolong_ref[...])
    up = dot_nt(ptop, top) + dot_nt(ptop, tail) + dot_nt(ptail, top)
    for part in range(3):
        lifted[part] = up[:, part * PL : (part + 1) * PL]


def correct_kernel(
    lifted, lift_ref, plane_ref, x1, xm, xp, x0, lw, mmat,
    field, wide, first, last,
    vhigh, vlow,
):
    plane = plane_tables(plane_ref)
    home = jnp.broadcast_to(lift_ref[0:1, :], (CF, PL))

    def raised(t, z):
        number = (t + 1) * 6 + z + 1
        return lanes_of(lifted[lax.div(number, 16)], home + CP * lax.rem(number, 16))

    def correct(index, carry):
        t, z = lax.div(index, 3), 2 * lax.rem(index, 3) - 1
        for column in range(2):
            site = place(t, z) + column
            field[site] = x1[site] + raised(t, z + column)
        return carry

    lax.fori_loop(0, 12, correct, 0)

    def correct_outside(z, carry):
        field[place(-1, z)] = xm[z] + raised(-1, z)
        field[place(4, z)] = xp[z] + raised(4, z)
        return carry

    lax.fori_loop(0, 4, correct_outside, 0)

    def finish(t, half, changes):
        for column, change in enumerate(changes):
            site = place(t, 2 * half + column)
            new = field[site] + x0[site] - change
            wide[site] = new
            (last if t else first)[2 * half + column] = new

    block_pairs((0, 3), mmat, field, lw, plane, vhigh, vlow, finish)


def rest_kernel(
    field, wide_in, first, last, plane_ref, x0, lw, mmat,
    wide, second, third, zlow, zhigh,
    vhigh, vlow,
):
    plane = plane_tables(plane_ref)
    halves_in_z = (zlow, zhigh)
    for half, target in enumerate(halves_in_z):
        target[0:2] = first[2 * half : 2 * half + 2]
        target[6:8] = last[2 * half : 2 * half + 2]

    def finish(t, half, changes):
        for column, change in enumerate(changes):
            site = place(t, 2 * half + column)
            new = field[site] + x0[site] - change
            wide[site] = new
            (second if t == 1 else third)[2 * half + column] = new
            halves_in_z[half][2 * t + column] = new

    block_pairs((1, 2), mmat, field, lw, plane, vhigh, vlow, finish)


def inner_kernel(wide_in, hzm, hzp, x0, lw, mmat, plane_ref, wide, x4, vhigh, vlow):
    plane = plane_tables(plane_ref)
    for t in range(4):
        wide[pl.ds(place(t, -2), 2)] = hzm[2 * t : 2 * t + 2]
        wide[pl.ds(place(t, 4), 2)] = hzp[2 * t : 2 * t + 2]

    blank_rows(wide, -1, 6)
    sweeps(6, edge_pair, mmat, wide, x0, lw, plane, vhigh, vlow, x4)
    sweeps(6, middle_pair, mmat, wide, x0, lw, plane, vhigh, vlow, x4)


def post_kernel(
    wide_in, x4_in, tm1, tm2, tp1, tp2, czm, czp, a0, a1, a2, a3, x0, lw, mmat, bmat, mhops, plane_ref,
    wide, x4, sol_out, res_out,
    vhigh, vlow, rest, sems,
):
    plane = plane_tables(plane_ref)
    for source, t in ((tm1, -1), (tm2, -2), (tp1, 4), (tp2, 5)):
        wide[pl.ds(place(t, 0), 4)] = source[...]
    for source, z in ((czm, -1), (czp, 4)):
        wide[place(-1, z)] = source[0]
        wide[place(4, z)] = source[1]

    close_edges(mhops, wide, lw, vhigh, vlow, x4)
    sweeps(4, outer_pair, mmat, wide, x0, lw, plane, vhigh, vlow, x4)

    def send(source, target, number, kind):
        copy = pltpu.make_async_copy(source, target.at[:, number, :], sems.at[kind, number])
        copy.start()
        return copy

    copies = [send(x4.at[place(n // 4, n % 4)], sol_out, n, 0) for n in range(16)]
    rows = (a0, a1, a2, a3)

    def finish(t, half, images):
        for column, image in enumerate(images):
            number = 4 * t + 2 * half + column
            rest[number] = rows[t][2 * half + column] - image
            copies.append(send(rest.at[number], res_out, number, 1))

    block_pairs(range(4), bmat, x4, lw, plane, vhigh, vlow, finish)
    for copy in copies:
        copy.wait()


STACKED = ((2, KF, 2 * PL), BF16)
FRAME = ((64, CF, PL), F32)
WEIGHTS = ((64, 8, PL), F32)
ROW = ((4, CF, PL), F32)
PAIRED = ((2 * CF, KF), BF16)


def call(kernel, outs, scratch, aliases, *args, limit=8, far=()):
    vmem, away = pl.BlockSpec(memory_space=pltpu.VMEM), pl.BlockSpec(memory_space=pl.ANY)
    return pl.pallas_call(
        kernel,
        out_shape=tuple(jax.ShapeDtypeStruct(shape, kind) for shape, kind in outs),
        in_specs=[vmem] * len(args),
        out_specs=tuple(away if number in far else vmem for number in range(len(outs))),
        scratch_shapes=[
            pltpu.VMEM(*entry) if isinstance(entry, tuple) else entry for entry in scratch
        ],
        input_output_aliases=aliases,
        compiler_params=pltpu.CompilerParams(vmem_limit_bytes=limit << 20),
    )(*args)


def moved(value, axes, step):
    count = 1
    for axis in axes if isinstance(axes, tuple) else (axes,):
        count *= lax.axis_size(axis)
    return lax.ppermute(value, axes, [(i, (i + step) % count) for i in range(count)])


def shards(
    rhs_field,
    link_weights,
    fine_blocks,
    smoother,
    plane_next,
    aggregate,
    restrict_map,
    prolong_map,
    coarse_blocks,
    coarse_smoother,
    coarse_next,
):
    rows = [jnp.transpose(rhs_field[0, :, t], (1, 0, 2)) for t in range(4)]
    lows, highs = (
        jnp.concatenate(
            [
                jnp.transpose(rhs_field[0, :, :, z : z + 2], (1, 2, 0, 3)),
                jnp.transpose(link_weights[:, :, z : z + 2], (1, 2, 0, 3)),
            ],
            axis=2,
        ).reshape(8, CF + 8, PL)
        for z in (0, 2)
    )
    ends = [
        jnp.concatenate([rows[t], jnp.transpose(link_weights[:, t], (1, 0, 2))], axis=1) for t in (0, 3)
    ]
    hzm, hzp = moved(highs, "gz", 1), moved(lows, "gz", -1)
    tm1, tp1 = moved(ends[1], TAXES, 1), moved(ends[0], TAXES, -1)
    ctm = moved(jnp.stack([hzm[7, 0:CF], hzp[6, 0:CF]]), TAXES, 1)
    ctp = moved(jnp.stack([hzm[1, 0:CF], hzp[0, 0:CF]]), TAXES, -1)

    hops = ((2, 2 * CF, CF), BF16)
    smat, mpair, bpair, cpair, csmat, mhops, bhops = call(
        prepare_kernel,
        (
            ((2 * CF, CF), BF16),
            PAIRED,
            PAIRED,
            ((2 * KC, 2 * CC), BF16),
            ((2 * CC, 2 * CC), BF16),
            hops,
            hops,
        ),
        (),
        {},
        smoother, fine_blocks, coarse_smoother, coarse_blocks,
    )
    member = (jnp.arange(16, dtype=jnp.int32)[:, None] == aggregate[None, :]).astype(F32)
    turn = jnp.broadcast_to(coarse_next[:, :, None], (4, CP, CC))
    home = jnp.broadcast_to(aggregate[None, :], (8, PL))

    x0, lw, x1 = call(
        local_kernel,
        (FRAME, WEIGHTS, FRAME),
        (STACKED, STACKED),
        {},
        *rows, link_weights.reshape(8, 16, PL), hzm, hzp, smat, mpair, plane_next,
    )
    (x1,) = call(edge_kernel, (FRAME,), (STACKED, STACKED), {2: 0}, x0, lw, x1, mpair, plane_next)
    x0, lw, x1, up, down, first, last = call(
        pre_kernel,
        (FRAME, WEIGHTS, FRAME, ((20, CP, CC), F32), ((20, CP, CC), F32), ROW, ROW),
        (STACKED, STACKED, ((24 * CP, CF), F32)),
        {15: 0, 16: 1, 17: 2},
        *rows, tm1, tp1, ctm, ctp, smat, bpair, mhops, bhops, restrict_map, plane_next, member,
        x0, lw, x1,
    )

    tcm, tcp = moved(up, TAXES, 1), moved(down, TAXES, -1)
    e2m, e2p = moved(up[16:20], TAXES, 2), moved(down[16:20], TAXES, -2)
    whole, tall = call(
        join_kernel,
        (((48, CP, CC), F32), ((40, CP, CC), F32)),
        (),
        {},
        up, down, tcm, tcp,
    )
    zcm, zcp = moved(tall, "gz", 1), moved(tall, "gz", -1)
    xm, xp = moved(last, TAXES, 1), moved(first, TAXES, -1)

    (lifted,) = call(
        coarse_kernel,
        (((3, CF, PL), F32),),
        (
            ((144, CP, CC), F32),
            ((144, CP, CC), F32),
            ((104 * CP, 2 * CC), BF16),
            ((76 * CP, 2 * KC), BF16),
        ),
        {},
        whole, e2m, e2p, zcm, zcp, csmat, cpair, turn, prolong_map.T,
        limit=12,
    )
    field, wide, r0, r3 = call(
        correct_kernel,
        (FRAME, FRAME, ROW, ROW),
        (STACKED, STACKED),
        {},
        lifted, home, plane_next, x1, xm, xp, x0, lw, mpair,
    )
    half = ((8, CF, PL), F32)
    wide, r1, r2, low, high = call(
        rest_kernel,
        (FRAME, ROW, ROW, half, half),
        (STACKED, STACKED),
        {1: 0},
        field, wide, r0, r3, plane_next, x0, lw, mpair,
    )
    tm1, tp1 = moved(r3, TAXES, 1), moved(r0, TAXES, -1)
    tm2, tp2 = moved(r2, TAXES, 1), moved(r1, TAXES, -1)
    hzm, hzp = moved(high, "gz", 1), moved(low, "gz", -1)
    czm = moved(jnp.stack([tm1[3], tp1[3]]), "gz", 1)
    czp = moved(jnp.stack([tm1[0], tp1[0]]), "gz", -1)
    wide, x4 = call(
        inner_kernel,
        (FRAME, FRAME),
        (STACKED, STACKED),
        {0: 0},
        wide, hzm, hzp, x0, lw, mpair, plane_next,
    )
    _, _, sol, res = call(
        post_kernel,
        (FRAME, FRAME, ((CF, 16, PL), F32), ((CF, 16, PL), F32)),
        (STACKED, STACKED, ((16, CF, PL), F32), pltpu.SemaphoreType.DMA((2, 16))),
        {0: 0, 1: 1},
        wide, x4, tm1, tm2, tp1, tp2, czm, czp, *rows, x0, lw, mpair, bpair, mhops, plane_next,
        far=(2, 3),
    )

    def natural(value):
        return value.reshape(1, CF, 4, 4, PL)

    return natural(sol), natural(res)


def solution(mesh):
    spread = P(None, None, TAXES, "gz", None)
    return jax.shard_map(
        shards,
        mesh=mesh,
        in_specs=(spread, P(None, TAXES, "gz", None)) + (P(),) * 9,
        out_specs=(spread, spread),
        check_vma=False,
    )
```

```python
import jax
import jax.numpy as jnp
from jax import lax
from jax.experimental import pallas as pl
from jax.experimental.pallas import tpu as pltpu
from jax.sharding import PartitionSpec as P


F32, BF16 = jnp.float32, jnp.bfloat16
CF, CC, PL, NB, CP = 96, 128, 128, 9, 8
KF, KC = NB * CF, NB * CC
SWEEPS = 3
TAXES = ("ta", "col")


def halves(value):
    high = value.astype(BF16)
    return high, (value - high.astype(F32)).astype(BF16)


def dot(left, right):
    return jnp.dot(left, right, preferred_element_type=F32)


def dot_nt(left, right):
    return lax.dot_general(left, right, (((1,), (1,)), ((), ())), preferred_element_type=F32)


def lanes_of(value, index):
    return jnp.take_along_axis(value, index, axis=1)


def side_by_side(ref, depth):
    return jnp.concatenate([ref[0, 0:depth, :], ref[1, 0:depth, :]], axis=1)


def product(matrix, high, low, depth=KF):
    both = dot(matrix[...], side_by_side(high, depth))
    return both[0:CF] + both[CF : 2 * CF] + dot(matrix[0:CF, :], side_by_side(low, depth))


def put(high, low, row, column, value):
    top, rest = halves(value)
    high[column, row : row + CF, :] = top
    low[column, row : row + CF, :] = rest


def fill(field, site, stride, weights, plane, high, low, column):
    here = field[site]
    put(high, low, 0, column, here)
    for hop, offset in enumerate((stride, -stride, 1, -1)):
        put(high, low, (hop + 1) * CF, column, field[site + offset] * weights[hop : hop + 1])
    for hop in range(4):
        there = lanes_of(here, plane[hop]) * weights[hop + 4 : hop + 5]
        put(high, low, (hop + 5) * CF, column, there)


def place(t, z):
    return (t + 2) * 8 + z + 2


def middle_pair(index):
    return 1 + lax.div(index, 3), 2 * lax.rem(index, 3) - 1


def edge_pair(index):
    return 3 * lax.div(index, 3), 2 * lax.rem(index, 3) - 1


def outer_pair(index):
    return 5 * lax.div(index, 2) - 1, 2 * lax.rem(index, 2)


def each(count, load, finish):
    load(0, 0)

    def body(index, carry):
        load(2 * index + 1, 1)
        finish(2 * index, 0)
        load(2 * index + 2, 0)
        finish(2 * index + 1, 1)
        return carry

    lax.fori_loop(0, count // 2 - 1, body, 0)
    load(count - 1, 1)
    finish(count - 2, 0)
    finish(count - 1, 1)


def plane_tables(ref):
    return [jnp.broadcast_to(ref[hop : hop + 1, :], (CF, PL)) for hop in range(4)]


def smooth(smat, high, low, x0, sources, targets):
    for column, source in enumerate(sources):
        put(high, low, 0, column, source)
    value = product(smat, high, low, CF)
    for column, target in enumerate(targets):
        x0[target] = value[:, column * PL : (column + 1) * PL]


def sweeps(count, where, matrix, field, x0, lw, plane, vhigh, vlow, target):
    def load(index, slot):
        site = place(*where(index))
        for column in range(2):
            fill(field, site + column, 8, lw[site + column], plane, vhigh.at[slot], vlow.at[slot], column)

    def finish(index, slot):
        site = place(*where(index))
        change = product(matrix, vhigh.at[slot], vlow.at[slot])
        for column in range(2):
            old = field[site + column] + x0[site + column]
            target[site + column] = old - change[:, column * PL : (column + 1) * PL]

    each(count, load, finish)


def block_pairs(rows, matrix, field, lw, plane, vhigh, vlow, finish):
    pairs = [(t, half) for t in rows for half in range(2)]

    def load(t, half):
        site = place(t, 2 * half)
        for column in range(2):
            fill(field, site + column, 8, lw[site + column], plane, vhigh.at[half], vlow.at[half], column)

    load(*pairs[0])
    for number, (t, half) in enumerate(pairs):
        if number + 1 < len(pairs):
            load(*pairs[number + 1])
        image = product(matrix, vhigh.at[half], vlow.at[half])
        finish(t, half, [image[:, 0:PL], image[:, PL : 2 * PL]])


def blank_rows(field, first, count):
    for t in (-1, 4):
        field[pl.ds(place(t, first), count)] = jnp.zeros((count, CF, PL), F32)


def one_hop(matrix, values, vhigh, vlow, slot):
    for column, value in enumerate(values):
        put(vhigh.at[slot], vlow.at[slot], 0, column, value)
    image = product(matrix, vhigh.at[slot], vlow.at[slot], CF)
    return [image[:, 0:PL], image[:, PL : 2 * PL]]


def close_edges(hops, field, lw, vhigh, vlow, target):
    for number, (t, outside, hop) in enumerate(((3, 4, 0), (0, -1, 1))):
        for pair in range(3):
            z = 2 * pair - 1
            here, there = place(t, z), place(outside, z)
            values = [field[there + c] * lw[here + c, hop : hop + 1, :] for c in range(2)]
            changes = one_hop(hops.at[hop], values, vhigh, vlow, (number + pair) % 2)
            for c in range(2):
                target[here + c] = target[here + c] - changes[c]


def exact_dot(left, right):
    parts = []
    for value in (left, right):
        top, rest = halves(value)
        tail = (value - top.astype(F32) - rest.astype(F32)).astype(BF16)
        parts.append((top, rest, tail))
    (l0, l1, l2), (r0, r1, r2) = parts
    small = dot(l0, r2) + dot(l1, r1) + dot(l2, r0)
    return small + (dot(l0, r1) + dot(l1, r0)) + dot(l0, r0)


def pair_matrix(target, row, depth, value):
    high, low = halves(value)
    target[row : row + CC, 0:CC] = high
    target[row : row + CC, CC : 2 * CC] = low
    target[depth + row : depth + row + CC, 0:CC] = high
    target[depth + row : depth + row + CC, CC : 2 * CC] = jnp.zeros((CC, CC), BF16)


def prepare_kernel(
    s_far, blocks_far, cs_far, coarse_far, r_far, prolong_far, plane_far, aggregate_far,
    smat, mmat, bmat, cmat, csmat, mhops, bhops, restrict, prolong, plane, home, member,
    s_ref, blocks, cs_ref, coarse, sems,
):
    copies = fetch(
        (
            (s_far, s_ref), (blocks_far, blocks), (cs_far, cs_ref), (coarse_far, coarse),
            (r_far, restrict), (prolong_far, prolong), (plane_far, plane), (aggregate_far, home),
        ),
        sems,
    )
    for copy in copies:
        copy.wait()
    rows = lax.broadcasted_iota(jnp.int32, (16, PL), 0)
    member[...] = (rows == jnp.broadcast_to(home[...], (16, PL))).astype(F32)
    smooth_matrix = s_ref[...]
    smat[0:CF, :], smat[CF : 2 * CF, :] = halves(smooth_matrix)
    whole = jnp.concatenate([blocks[k] for k in range(NB)], axis=1)
    bmat[0:CF, :], bmat[CF : 2 * CF, :] = halves(whole)
    mmat[0:CF, :], mmat[CF : 2 * CF, :] = halves(exact_dot(smooth_matrix, whole))
    for hop in range(2):
        block = blocks[hop + 1]
        bhops[hop, 0:CF, :], bhops[hop, CF : 2 * CF, :] = halves(block)
        mhops[hop, 0:CF, :], mhops[hop, CF : 2 * CF, :] = halves(exact_dot(smooth_matrix, block))
    coarse_smooth = cs_ref[...]
    for k in range(NB):
        pair_matrix(cmat, k * CC, KC, jnp.transpose(exact_dot(coarse_smooth, coarse[k]), (1, 0)))
    pair_matrix(csmat, 0, CC, jnp.transpose(coarse_smooth, (1, 0)))


def fetch(pairs, sems):
    copies = [pltpu.make_async_copy(source, target, sems.at[n]) for n, (source, target) in enumerate(pairs)]
    for copy in copies:
        copy.start()
    return copies


def pack_kernel(rhs_far, weights_far, low, high, a0, a1, a2, a3, by_site, rhs, weights, sems):
    for copy in fetch(((weights_far, weights), (rhs_far, rhs)), sems):
        copy.wait()
    for t, row in enumerate((a0, a1, a2, a3)):
        for z in range(4):
            field = rhs[pl.ds(4 * t + z, CF, stride=16), :]
            links = weights[pl.ds(4 * t + z, 8, stride=16), :]
            half, number = (high if z >= 2 else low), 2 * t + z % 2
            half[number, 0:CF, :] = field
            half[number, CF : CF + 8, :] = links
            by_site[4 * t + z] = links
            row[z, 0:CF, :] = field
            if t in (0, 3):
                row[z, CF : CF + 8, :] = links


def local_kernel(
    a0, a1, a2, a3, l_ref, hzm, hzp, smat, mmat, plane_ref,
    x0, lw, x1,
    vhigh, vlow,
):
    plane = plane_tables(plane_ref)
    for t, row in enumerate((a0, a1, a2, a3)):
        for pair in range(2):
            site = place(t, 2 * pair)
            slot = pair
            smooth(smat, vhigh.at[slot], vlow.at[slot], x0, [row[2 * pair, 0:CF, :], row[2 * pair + 1, 0:CF, :]], [site, site + 1])
        lw[pl.ds(place(t, 0), 4)] = l_ref[4 * t : 4 * t + 4]
        for slot, (source, z) in enumerate(((hzm, -2), (hzp, 4))):
            site = place(t, z)
            smooth(
                smat, vhigh.at[slot], vlow.at[slot], x0,
                [source[2 * t, 0:CF, :], source[2 * t + 1, 0:CF, :]], [site, site + 1],
            )
        lw[place(t, -1)] = hzm[2 * t + 1, CF : CF + 8, :]
        lw[place(t, 4)] = hzp[2 * t, CF : CF + 8, :]

    blank_rows(x0, -1, 6)
    blank_rows(x1, 0, 4)
    sweeps(6, middle_pair, mmat, x0, x0, lw, plane, vhigh, vlow, x1)


def edge_kernel(x0, lw, x1_in, mmat, plane_ref, x1, vhigh, vlow):
    plane = plane_tables(plane_ref)
    sweeps(6, edge_pair, mmat, x0, x0, lw, plane, vhigh, vlow, x1)


def pre_kernel(
    a0, a1, a2, a3, tm1, tp1, ctm, ctp, smat, bmat, mhops, bhops, r_ref, plane_ref, member_ref,
    x0_in, lw_in, x1_in,
    x0, lw, x1, up_out, down_out, first_out, last_out,
    vhigh, vlow, summed,
):
    plane = plane_tables(plane_ref)
    for source, t in ((tm1, -1), (tp1, 4)):
        for slot in range(2):
            site = place(t, 2 * slot)
            smooth(
                smat, vhigh.at[slot], vlow.at[slot], x0,
                [source[2 * slot, 0:CF, :], source[2 * slot + 1, 0:CF, :]], [site, site + 1],
            )
        lw[pl.ds(place(t, 0), 4)] = source[:, CF : CF + 8, :]
    for slot, (source, t) in enumerate(((ctm, -1), (ctp, 4))):
        smooth(
            smat, vhigh.at[slot], vlow.at[slot], x0,
            [source[0], source[1]], [place(t, -1), place(t, 4)],
        )

    close_edges(mhops, x0, lw, vhigh, vlow, x1)
    first_out[...] = x1[pl.ds(place(0, 0), 4)]
    last_out[...] = x1[pl.ds(place(3, 0), 4)]

    member = member_ref[...].astype(BF16)
    rows = (a0, a1, a2, a3)

    def restrict(number, value):
        top, tail = halves(value)
        total = dot_nt(member, top) + dot_nt(member, tail)
        summed[number * 8 : number * 8 + 8, :] = total[0:8]

    def finish(t, half, images):
        for column, image in enumerate(images):
            restrict(4 * t + 2 * half + column, rows[t][2 * half + column, 0:CF, :] - image)

    block_pairs(range(4), bmat, x1, lw, plane, vhigh, vlow, finish)
    for base, t, outside, hop in ((16, 3, 4, 1), (20, 0, -1, 0)):
        for half in range(2):
            here, there = place(t, 2 * half), place(outside, 2 * half)
            values = [x1[here + c] * lw[there + c, hop : hop + 1, :] for c in range(2)]
            images = one_hop(bhops.at[hop], values, vhigh, vlow, half)
            for c in range(2):
                restrict(base + 2 * half + c, -images[c])
    top, tail = halves(summed[...])
    rtop, rtail = halves(r_ref[...])
    crhs = dot(top, rtop) + dot(tail, rtop) + dot(top, rtail)
    crhs = crhs.reshape(24, CP, CC)
    up_out[...] = crhs[0:20]
    down_out[0:16] = crhs[0:16]
    down_out[16:20] = crhs[20:24]


def join_kernel(up, down, tcm, tcp, whole, tall):
    whole[0:16] = tcm[0:16]
    whole[12:16] = tcm[12:16] + down[16:20]
    whole[16:32] = up[0:16]
    whole[16:20] = up[0:4] + tcm[16:20]
    whole[28:32] = up[12:16] + tcp[16:20]
    whole[32:48] = tcp[0:16]
    whole[32:36] = tcp[0:4] + up[16:20]
    tall[...] = whole[4:44]


def diamond(radius):
    rows = []
    for t in range(-radius, 4 + radius):
        reach = radius - max(0, -t, t - 3)
        rows.append((t, -reach, 4 + 2 * reach))
    return rows


def coarse_kernel(
    whole, e2m, e2p, zcm, zcp, csmat, cmat, coarse_ref, prolong_ref,
    lifted,
    w0, w, packed, operand,
):
    for t in range(12):
        own = whole[4 * t : 4 * t + 4]
        if t in (0, 11):
            own = own + (e2p if t else e2m)[...]
        w[pl.ds(t * 12 + 4, 4)] = own
        side = t - 1
        if 0 <= side < 10:
            w[pl.ds(t * 12, 4)] = zcm[4 * side : 4 * side + 4]
            w[pl.ds(t * 12 + 8, 4)] = zcp[4 * side : 4 * side + 4]

    def spot(t, z):
        return (t + 4) * 12 + z + 4

    row = 0
    for t, z, count in diamond(4):
        size = count * CP
        top, tail = halves(w[pl.ds(spot(t, z), count)].reshape(size, CC))
        packed[row : row + size, 0:CC] = top
        packed[row : row + size, CC : 2 * CC] = tail
        row += size
    both = dot(packed[...], csmat[...])
    first = both[:, 0:CC] + both[:, CC : 2 * CC]
    row = 0
    for t, z, count in diamond(4):
        size = count * CP
        value = first[row : row + size].reshape(count, CP, CC)
        w0[pl.ds(spot(t, z), count)] = value
        w[pl.ds(spot(t, z), count)] = value
        row += size
    turn = [coarse_ref[hop] for hop in range(4)]

    for sweep in range(SWEEPS):
        shape = diamond(SWEEPS - sweep)
        row = 0
        for t, z, count in shape:
            size = count * CP
            start = spot(t, z)
            blocks = [w[pl.ds(start + offset, count)].reshape(size, CC) for offset in (0, 12, -12, 1, -1)]
            for hop in range(4):
                blocks.append(
                    jnp.concatenate(
                        [jnp.take_along_axis(w[start + n], turn[hop], axis=0) for n in range(count)], axis=0
                    )
                )
            for hop, block in enumerate(blocks):
                top, tail = halves(block)
                operand[row : row + size, hop * CC : (hop + 1) * CC] = top
                operand[row : row + size, KC + hop * CC : KC + (hop + 1) * CC] = tail
            row += size
        both = dot(operand[0:row, :], cmat[...])
        change = both[:, 0:CC] + both[:, CC : 2 * CC]
        row = 0
        for t, z, count in shape:
            size = count * CP
            place_of = pl.ds(spot(t, z), count)
            w[place_of] = w[place_of] + w0[place_of] - change[row : row + size].reshape(count, CP, CC)
            row += size

    near = jnp.concatenate([w[pl.ds(spot(t, -1), 6)] for t in range(-1, 5)], axis=0)
    near = jnp.concatenate([near.reshape(36 * CP, CC), jnp.zeros((12 * CP, CC), F32)], axis=0)
    top, tail = halves(near)
    ptop, ptail = halves(prolong_ref[...])
    up = dot_nt(ptop, top) + dot_nt(ptop, tail) + dot_nt(ptail, top)
    for part in range(3):
        lifted[part] = up[:, part * PL : (part + 1) * PL]


def correct_kernel(
    lifted, lift_ref, plane_ref, x1, xm, xp, x0, lw, mmat,
    field, wide, first, last,
    vhigh, vlow,
):
    plane = plane_tables(plane_ref)
    home = jnp.broadcast_to(lift_ref[0:1, :], (CF, PL))

    def raised(t, z):
        number = (t + 1) * 6 + z + 1
        return lanes_of(lifted[lax.div(number, 16)], home + CP * lax.rem(number, 16))

    def correct(index, carry):
        t, z = lax.div(index, 3), 2 * lax.rem(index, 3) - 1
        for column in range(2):
            site = place(t, z) + column
            field[site] = x1[site] + raised(t, z + column)
        return carry

    lax.fori_loop(0, 12, correct, 0)

    def correct_outside(z, carry):
        field[place(-1, z)] = xm[z] + raised(-1, z)
        field[place(4, z)] = xp[z] + raised(4, z)
        return carry

    lax.fori_loop(0, 4, correct_outside, 0)

    def finish(t, half, changes):
        for column, change in enumerate(changes):
            site = place(t, 2 * half + column)
            new = field[site] + x0[site] - change
            wide[site] = new
            (last if t else first)[2 * half + column] = new

    block_pairs((0, 3), mmat, field, lw, plane, vhigh, vlow, finish)


def rest_kernel(
    field, wide_in, first, last, plane_ref, x0, lw, mmat,
    wide, second, third, zlow, zhigh,
    vhigh, vlow,
):
    plane = plane_tables(plane_ref)
    halves_in_z = (zlow, zhigh)
    for half, target in enumerate(halves_in_z):
        target[0:2] = first[2 * half : 2 * half + 2]
        target[6:8] = last[2 * half : 2 * half + 2]

    def finish(t, half, changes):
        for column, change in enumerate(changes):
            site = place(t, 2 * half + column)
            new = field[site] + x0[site] - change
            wide[site] = new
            (second if t == 1 else third)[2 * half + column] = new
            halves_in_z[half][2 * t + column] = new

    block_pairs((1, 2), mmat, field, lw, plane, vhigh, vlow, finish)


def inner_kernel(wide_in, hzm, hzp, x0, lw, mmat, plane_ref, wide, x4, vhigh, vlow):
    plane = plane_tables(plane_ref)
    for t in range(4):
        wide[pl.ds(place(t, -2), 2)] = hzm[2 * t : 2 * t + 2]
        wide[pl.ds(place(t, 4), 2)] = hzp[2 * t : 2 * t + 2]

    blank_rows(wide, -1, 6)
    sweeps(6, edge_pair, mmat, wide, x0, lw, plane, vhigh, vlow, x4)
    sweeps(6, middle_pair, mmat, wide, x0, lw, plane, vhigh, vlow, x4)


def post_kernel(
    wide_in, x4_in, tm1, tm2, tp1, tp2, czm, czp, a0, a1, a2, a3, x0, lw, mmat, bmat, mhops, plane_ref,
    wide, x4, sol_out, res_out,
    vhigh, vlow, rest, sems,
):
    plane = plane_tables(plane_ref)
    for source, t in ((tm1, -1), (tm2, -2), (tp1, 4), (tp2, 5)):
        wide[pl.ds(place(t, 0), 4)] = source[...]
    for source, z in ((czm, -1), (czp, 4)):
        wide[place(-1, z)] = source[0]
        wide[place(4, z)] = source[1]

    close_edges(mhops, wide, lw, vhigh, vlow, x4)
    sweeps(4, outer_pair, mmat, wide, x0, lw, plane, vhigh, vlow, x4)

    def send(source, target, number, kind):
        copy = pltpu.make_async_copy(source, target.at[:, number, :], sems.at[kind, number])
        copy.start()
        return copy

    copies = [send(x4.at[place(n // 4, n % 4)], sol_out, n, 0) for n in range(16)]
    rows = (a0, a1, a2, a3)

    def finish(t, half, images):
        for column, image in enumerate(images):
            number = 4 * t + 2 * half + column
            rest[number] = rows[t][2 * half + column, 0:CF, :] - image
            copies.append(send(rest.at[number], res_out, number, 1))

    block_pairs(range(4), bmat, x4, lw, plane, vhigh, vlow, finish)
    for copy in copies:
        copy.wait()


STACKED = ((2, 2, KF, PL), BF16)
FRAME = ((64, CF, PL), F32)
WEIGHTS = ((64, 8, PL), F32)
ROW = ((4, CF, PL), F32)
PAIRED = ((2 * CF, KF), BF16)


def call(kernel, outs, scratch, aliases, *args, limit=8, far=(), away=()):
    vmem, hbm = pl.BlockSpec(memory_space=pltpu.VMEM), pl.BlockSpec(memory_space=pltpu.HBM)
    built = pl.pallas_call(
        kernel,
        out_shape=tuple(jax.ShapeDtypeStruct(shape, kind) for shape, kind in outs),
        in_specs=[hbm if number in away else vmem for number in range(len(args))],
        out_specs=tuple(hbm if number in far else vmem for number in range(len(outs))),
        scratch_shapes=[
            pltpu.VMEM(*entry) if isinstance(entry, tuple) else entry for entry in scratch
        ],
        input_output_aliases=aliases,
        compiler_params=pltpu.CompilerParams(vmem_limit_bytes=limit << 20),
    )
    args = [
        pltpu.with_memory_space_constraint(value, pltpu.HBM) if number in away else value
        for number, value in enumerate(args)
    ]
    return built(*args)


def moved(value, axes, step):
    count = 1
    for axis in axes if isinstance(axes, tuple) else (axes,):
        count *= lax.axis_size(axis)
    return lax.ppermute(value, axes, [(i, (i + step) % count) for i in range(count)])


def shards(
    rhs_field,
    link_weights,
    fine_blocks,
    smoother,
    plane_next,
    aggregate,
    restrict_map,
    prolong_map,
    coarse_blocks,
    coarse_smoother,
    coarse_next,
):
    near = ((4, CF + 8, PL), F32)
    sides = ((8, CF + 8, PL), F32)
    lows, highs, *rows, links = call(
        pack_kernel,
        (sides, sides, near, ROW, ROW, near, ((16, 8, PL), F32)),
        (((CF * 16, PL), F32), ((8 * 16, PL), F32), pltpu.SemaphoreType.DMA((2,))),
        {},
        rhs_field.reshape(CF * 16, PL), link_weights.reshape(8 * 16, PL),
        away=(0, 1),
    )
    hzm, hzp = moved(highs, "gz", 1), moved(lows, "gz", -1)
    tm1, tp1 = moved(rows[3], TAXES, 1), moved(rows[0], TAXES, -1)
    ctm = moved(jnp.stack([hzm[7, 0:CF], hzp[6, 0:CF]]), TAXES, 1)
    ctp = moved(jnp.stack([hzm[1, 0:CF], hzp[0, 0:CF]]), TAXES, -1)

    hops = ((2, 2 * CF, CF), BF16)
    smat, mpair, bpair, cpair, csmat, mhops, bhops, restrict, prolong, plane, home, member = call(
        prepare_kernel,
        (
            ((2 * CF, CF), BF16),
            PAIRED,
            PAIRED,
            ((2 * KC, 2 * CC), BF16),
            ((2 * CC, 2 * CC), BF16),
            hops,
            hops,
            ((CF, CC), F32),
            ((CF, CC), F32),
            ((4, PL), jnp.int32),
            ((1, PL), jnp.int32),
            ((16, PL), F32),
        ),
        (
            ((CF, CF), F32),
            ((NB, CF, CF), F32),
            ((CC, CC), F32),
            ((NB, CC, CC), F32),
            pltpu.SemaphoreType.DMA((8,)),
        ),
        {},
        smoother, fine_blocks, coarse_smoother, coarse_blocks, restrict_map, prolong_map.T, plane_next,
        aggregate.reshape(1, PL),
        away=range(8),
    )
    turn = jnp.broadcast_to(coarse_next[:, :, None], (4, CP, CC))

    x0, lw, x1 = call(
        local_kernel,
        (FRAME, WEIGHTS, FRAME),
        (STACKED, STACKED),
        {},
        *rows, links, hzm, hzp, smat, mpair, plane,
    )
    (x1,) = call(edge_kernel, (FRAME,), (STACKED, STACKED), {2: 0}, x0, lw, x1, mpair, plane)
    x0, lw, x1, up, down, first, last = call(
        pre_kernel,
        (FRAME, WEIGHTS, FRAME, ((20, CP, CC), F32), ((20, CP, CC), F32), ROW, ROW),
        (STACKED, STACKED, ((24 * CP, CF), F32)),
        {15: 0, 16: 1, 17: 2},
        *rows, tm1, tp1, ctm, ctp, smat, bpair, mhops, bhops, restrict, plane, member,
        x0, lw, x1,
    )

    tcm, tcp = moved(up, TAXES, 1), moved(down, TAXES, -1)
    e2m, e2p = moved(up[16:20], TAXES, 2), moved(down[16:20], TAXES, -2)
    whole, tall = call(
        join_kernel,
        (((48, CP, CC), F32), ((40, CP, CC), F32)),
        (),
        {},
        up, down, tcm, tcp,
    )
    zcm, zcp = moved(tall, "gz", 1), moved(tall, "gz", -1)
    xm, xp = moved(last, TAXES, 1), moved(first, TAXES, -1)

    (lifted,) = call(
        coarse_kernel,
        (((3, CF, PL), F32),),
        (
            ((144, CP, CC), F32),
            ((144, CP, CC), F32),
            ((104 * CP, 2 * CC), BF16),
            ((76 * CP, 2 * KC), BF16),
        ),
        {},
        whole, e2m, e2p, zcm, zcp, csmat, cpair, turn, prolong,
        limit=12,
    )
    field, wide, r0, r3 = call(
        correct_kernel,
        (FRAME, FRAME, ROW, ROW),
        (STACKED, STACKED),
        {},
        lifted, home, plane, x1, xm, xp, x0, lw, mpair,
    )
    half = ((8, CF, PL), F32)
    wide, r1, r2, low, high = call(
        rest_kernel,
        (FRAME, ROW, ROW, half, half),
        (STACKED, STACKED),
        {1: 0},
        field, wide, r0, r3, plane, x0, lw, mpair,
    )
    tm1, tp1 = moved(r3, TAXES, 1), moved(r0, TAXES, -1)
    tm2, tp2 = moved(r2, TAXES, 1), moved(r1, TAXES, -1)
    hzm, hzp = moved(high, "gz", 1), moved(low, "gz", -1)
    czm = moved(jnp.stack([tm1[3], tp1[3]]), "gz", 1)
    czp = moved(jnp.stack([tm1[0], tp1[0]]), "gz", -1)
    wide, x4 = call(
        inner_kernel,
        (FRAME, FRAME),
        (STACKED, STACKED),
        {0: 0},
        wide, hzm, hzp, x0, lw, mpair, plane,
    )
    _, _, sol, res = call(
        post_kernel,
        (FRAME, FRAME, ((CF, 16, PL), F32), ((CF, 16, PL), F32)),
        (STACKED, STACKED, ((16, CF, PL), F32), pltpu.SemaphoreType.DMA((2, 16))),
        {0: 0, 1: 1},
        wide, x4, tm1, tm2, tp1, tp2, czm, czp, *rows, x0, lw, mpair, bpair, mhops, plane,
        far=(2, 3),
    )

    def natural(value):
        return value.reshape(1, CF, 4, 4, PL)

    return natural(sol), natural(res)


def solution(mesh):
    spread = P(None, None, TAXES, "gz", None)
    return jax.shard_map(
        shards,
        mesh=mesh,
        in_specs=(spread, P(None, TAXES, "gz", None)) + (P(),) * 9,
        out_specs=(spread, spread),
        check_vma=False,
    )
```

```python
import jax
import jax.numpy as jnp
from jax import lax
from jax.experimental import pallas as pl
from jax.experimental.pallas import tpu as pltpu
from jax.sharding import PartitionSpec as P


F32, BF16 = jnp.float32, jnp.bfloat16
CF, CC, PL, NB, CP = 96, 128, 128, 9, 8
KF, KC = NB * CF, NB * CC
SWEEPS = 3
TAXES = ("ta", "col")


def halves(value):
    high = value.astype(BF16)
    return high, (value - high.astype(F32)).astype(BF16)


def dot(left, right):
    return jnp.dot(left, right, preferred_element_type=F32)


def dot_nt(left, right):
    return lax.dot_general(left, right, (((1,), (1,)), ((), ())), preferred_element_type=F32)


def lanes_of(value, index):
    return jnp.take_along_axis(value, index, axis=1)


def side_by_side(ref, depth):
    return jnp.concatenate([ref[0, 0:depth, :], ref[1, 0:depth, :]], axis=1)


def product(matrix, high, low, depth=KF):
    both = dot(matrix[...], side_by_side(high, depth))
    return both[0:CF] + both[CF : 2 * CF] + dot(matrix[0:CF, :], side_by_side(low, depth))


def put(high, low, row, column, value):
    top, rest = halves(value)
    high[column, row : row + CF, :] = top
    low[column, row : row + CF, :] = rest


def fill(field, site, stride, weights, plane, high, low, column):
    here = field[site]
    put(high, low, 0, column, here)
    for hop, offset in enumerate((stride, -stride, 1, -1)):
        put(high, low, (hop + 1) * CF, column, field[site + offset] * weights[hop : hop + 1])
    for hop in range(4):
        there = lanes_of(here, plane[hop]) * weights[hop + 4 : hop + 5]
        put(high, low, (hop + 5) * CF, column, there)


def place(t, z):
    return (t + 2) * 8 + z + 2


def middle_pair(index):
    return 1 + lax.div(index, 3), 2 * lax.rem(index, 3) - 1


def edge_pair(index):
    return 3 * lax.div(index, 3), 2 * lax.rem(index, 3) - 1


def outer_pair(index):
    return 5 * lax.div(index, 2) - 1, 2 * lax.rem(index, 2)


def each(count, load, finish):
    load(0, 0)

    def body(index, carry):
        load(2 * index + 1, 1)
        finish(2 * index, 0)
        load(2 * index + 2, 0)
        finish(2 * index + 1, 1)
        return carry

    lax.fori_loop(0, count // 2 - 1, body, 0)
    load(count - 1, 1)
    finish(count - 2, 0)
    finish(count - 1, 1)


def plane_tables(ref):
    return [jnp.broadcast_to(ref[hop : hop + 1, :], (CF, PL)) for hop in range(4)]


def smooth(smat, high, low, x0, sources, targets):
    for column, source in enumerate(sources):
        put(high, low, 0, column, source)
    value = product(smat, high, low, CF)
    for column, target in enumerate(targets):
        x0[target] = value[:, column * PL : (column + 1) * PL]


def sweeps(count, where, matrix, field, x0, lw, plane, vhigh, vlow, target):
    def load(index, slot):
        site = place(*where(index))
        for column in range(2):
            fill(field, site + column, 8, lw[site + column], plane, vhigh.at[slot], vlow.at[slot], column)

    def finish(index, slot):
        site = place(*where(index))
        change = product(matrix, vhigh.at[slot], vlow.at[slot])
        for column in range(2):
            old = field[site + column] + x0[site + column]
            target[site + column] = old - change[:, column * PL : (column + 1) * PL]

    each(count, load, finish)


def block_pairs(rows, matrix, field, lw, plane, vhigh, vlow, finish):
    pairs = [(t, half) for t in rows for half in range(2)]

    def load(t, half):
        site = place(t, 2 * half)
        for column in range(2):
            fill(field, site + column, 8, lw[site + column], plane, vhigh.at[half], vlow.at[half], column)

    load(*pairs[0])
    for number, (t, half) in enumerate(pairs):
        if number + 1 < len(pairs):
            load(*pairs[number + 1])
        image = product(matrix, vhigh.at[half], vlow.at[half])
        finish(t, half, [image[:, 0:PL], image[:, PL : 2 * PL]])


def blank_rows(field, first, count):
    for t in (-1, 4):
        field[pl.ds(place(t, first), count)] = jnp.zeros((count, CF, PL), F32)


def one_hop(matrix, values, vhigh, vlow, slot):
    for column, value in enumerate(values):
        put(vhigh.at[slot], vlow.at[slot], 0, column, value)
    image = product(matrix, vhigh.at[slot], vlow.at[slot], CF)
    return [image[:, 0:PL], image[:, PL : 2 * PL]]


def close_edges(hops, field, lw, vhigh, vlow, target):
    for number, (t, outside, hop) in enumerate(((3, 4, 0), (0, -1, 1))):
        for pair in range(3):
            z = 2 * pair - 1
            here, there = place(t, z), place(outside, z)
            values = [field[there + c] * lw[here + c, hop : hop + 1, :] for c in range(2)]
            changes = one_hop(hops.at[hop], values, vhigh, vlow, (number + pair) % 2)
            for c in range(2):
                target[here + c] = target[here + c] - changes[c]


def exact_dot(left, right):
    parts = []
    for value in (left, right):
        top, rest = halves(value)
        tail = (value - top.astype(F32) - rest.astype(F32)).astype(BF16)
        parts.append((top, rest, tail))
    (l0, l1, l2), (r0, r1, r2) = parts
    small = dot(l0, r2) + dot(l1, r1) + dot(l2, r0)
    return small + (dot(l0, r1) + dot(l1, r0)) + dot(l0, r0)


def pair_matrix(target, row, depth, value):
    high, low = halves(value)
    target[row : row + CC, 0:CC] = high
    target[row : row + CC, CC : 2 * CC] = low
    target[depth + row : depth + row + CC, 0:CC] = high
    target[depth + row : depth + row + CC, CC : 2 * CC] = jnp.zeros((CC, CC), BF16)


def prepare_kernel(s_ref, blocks, home, smat, mmat, bmat, mhops, bhops, member):
    rows = lax.broadcasted_iota(jnp.int32, (16, PL), 0)
    member[...] = (rows == jnp.broadcast_to(home[...], (16, PL))).astype(F32)
    smooth_matrix = s_ref[...]
    smat[0:CF, :], smat[CF : 2 * CF, :] = halves(smooth_matrix)
    whole = jnp.concatenate([blocks[k] for k in range(NB)], axis=1)
    bmat[0:CF, :], bmat[CF : 2 * CF, :] = halves(whole)
    mmat[0:CF, :], mmat[CF : 2 * CF, :] = halves(exact_dot(smooth_matrix, whole))
    for hop in range(2):
        block = blocks[hop + 1]
        bhops[hop, 0:CF, :], bhops[hop, CF : 2 * CF, :] = halves(block)
        mhops[hop, 0:CF, :], mhops[hop, CF : 2 * CF, :] = halves(exact_dot(smooth_matrix, block))


def ready_kernel(cs_far, coarse_far, prolong_far, cmat, csmat, prolong, cs_ref, coarse, sems):
    copies = fetch(((cs_far, cs_ref), (coarse_far, coarse), (prolong_far, prolong)), sems)
    for copy in copies:
        copy.wait()
    coarse_smooth = cs_ref[...]
    for k in range(NB):
        pair_matrix(cmat, k * CC, KC, jnp.transpose(exact_dot(coarse_smooth, coarse[k]), (1, 0)))
    pair_matrix(csmat, 0, CC, jnp.transpose(coarse_smooth, (1, 0)))


def fetch(pairs, sems):
    copies = [pltpu.make_async_copy(source, target, sems.at[n]) for n, (source, target) in enumerate(pairs)]
    for copy in copies:
        copy.start()
    return copies


def pack_kernel(
    rhs_far, weights_far, s_far, blocks_far, r_far, plane_far, aggregate_far,
    low, high, a0, a1, a2, a3, by_site, s_ref, blocks, restrict, plane, home,
    rhs, weights, sems,
):
    copies = fetch(
        (
            (weights_far, weights), (rhs_far, rhs), (s_far, s_ref), (blocks_far, blocks),
            (r_far, restrict), (plane_far, plane), (aggregate_far, home),
        ),
        sems,
    )
    copies[0].wait()
    copies[1].wait()
    for t, row in enumerate((a0, a1, a2, a3)):
        for z in range(4):
            field = rhs[pl.ds(4 * t + z, CF, stride=16), :]
            links = weights[pl.ds(4 * t + z, 8, stride=16), :]
            half, number = (high if z >= 2 else low), 2 * t + z % 2
            half[number, 0:CF, :] = field
            half[number, CF : CF + 8, :] = links
            by_site[4 * t + z] = links
            row[z, 0:CF, :] = field
            if t in (0, 3):
                row[z, CF : CF + 8, :] = links
    for copy in copies[2:]:
        copy.wait()


def local_kernel(
    a0, a1, a2, a3, l_ref, hzm, hzp, smat, mmat, plane_ref,
    x0, lw, x1,
    vhigh, vlow,
):
    plane = plane_tables(plane_ref)
    for t, row in enumerate((a0, a1, a2, a3)):
        for pair in range(2):
            site = place(t, 2 * pair)
            slot = pair
            smooth(smat, vhigh.at[slot], vlow.at[slot], x0, [row[2 * pair, 0:CF, :], row[2 * pair + 1, 0:CF, :]], [site, site + 1])
        lw[pl.ds(place(t, 0), 4)] = l_ref[4 * t : 4 * t + 4]
        for slot, (source, z) in enumerate(((hzm, -2), (hzp, 4))):
            site = place(t, z)
            smooth(
                smat, vhigh.at[slot], vlow.at[slot], x0,
                [source[2 * t, 0:CF, :], source[2 * t + 1, 0:CF, :]], [site, site + 1],
            )
        lw[place(t, -1)] = hzm[2 * t + 1, CF : CF + 8, :]
        lw[place(t, 4)] = hzp[2 * t, CF : CF + 8, :]

    blank_rows(x0, -1, 6)
    blank_rows(x1, 0, 4)
    sweeps(6, middle_pair, mmat, x0, x0, lw, plane, vhigh, vlow, x1)


def edge_kernel(x0, lw, x1_in, mmat, plane_ref, x1, vhigh, vlow):
    plane = plane_tables(plane_ref)
    sweeps(6, edge_pair, mmat, x0, x0, lw, plane, vhigh, vlow, x1)


def pre_kernel(
    a0, a1, a2, a3, tm1, tp1, ctm, ctp, smat, bmat, mhops, bhops, r_ref, plane_ref, member_ref,
    x0_in, lw_in, x1_in,
    x0, lw, x1, up_out, down_out, first_out, last_out,
    vhigh, vlow, summed,
):
    plane = plane_tables(plane_ref)
    for source, t in ((tm1, -1), (tp1, 4)):
        for slot in range(2):
            site = place(t, 2 * slot)
            smooth(
                smat, vhigh.at[slot], vlow.at[slot], x0,
                [source[2 * slot, 0:CF, :], source[2 * slot + 1, 0:CF, :]], [site, site + 1],
            )
        lw[pl.ds(place(t, 0), 4)] = source[:, CF : CF + 8, :]
    for slot, (source, t) in enumerate(((ctm, -1), (ctp, 4))):
        smooth(
            smat, vhigh.at[slot], vlow.at[slot], x0,
            [source[0], source[1]], [place(t, -1), place(t, 4)],
        )

    close_edges(mhops, x0, lw, vhigh, vlow, x1)
    first_out[...] = x1[pl.ds(place(0, 0), 4)]
    last_out[...] = x1[pl.ds(place(3, 0), 4)]

    member = member_ref[...].astype(BF16)
    rows = (a0, a1, a2, a3)

    def restrict(number, value):
        top, tail = halves(value)
        total = dot_nt(member, top) + dot_nt(member, tail)
        summed[number * 8 : number * 8 + 8, :] = total[0:8]

    def finish(t, half, images):
        for column, image in enumerate(images):
            restrict(4 * t + 2 * half + column, rows[t][2 * half + column, 0:CF, :] - image)

    block_pairs(range(4), bmat, x1, lw, plane, vhigh, vlow, finish)
    for base, t, outside, hop in ((16, 3, 4, 1), (20, 0, -1, 0)):
        for half in range(2):
            here, there = place(t, 2 * half), place(outside, 2 * half)
            values = [x1[here + c] * lw[there + c, hop : hop + 1, :] for c in range(2)]
            images = one_hop(bhops.at[hop], values, vhigh, vlow, half)
            for c in range(2):
                restrict(base + 2 * half + c, -images[c])
    top, tail = halves(summed[...])
    rtop, rtail = halves(r_ref[...])
    crhs = dot(top, rtop) + dot(tail, rtop) + dot(top, rtail)
    crhs = crhs.reshape(24, CP, CC)
    up_out[...] = crhs[0:20]
    down_out[0:16] = crhs[0:16]
    down_out[16:20] = crhs[20:24]


def join_kernel(up, down, tcm, tcp, whole, tall):
    whole[0:16] = tcm[0:16]
    whole[12:16] = tcm[12:16] + down[16:20]
    whole[16:32] = up[0:16]
    whole[16:20] = up[0:4] + tcm[16:20]
    whole[28:32] = up[12:16] + tcp[16:20]
    whole[32:48] = tcp[0:16]
    whole[32:36] = tcp[0:4] + up[16:20]
    tall[...] = whole[4:44]


def diamond(radius):
    rows = []
    for t in range(-radius, 4 + radius):
        reach = radius - max(0, -t, t - 3)
        rows.append((t, -reach, 4 + 2 * reach))
    return rows


def coarse_kernel(
    whole, e2m, e2p, zcm, zcp, csmat, cmat, coarse_ref, prolong_ref,
    lifted,
    w0, w, packed, operand,
):
    for t in range(12):
        own = whole[4 * t : 4 * t + 4]
        if t in (0, 11):
            own = own + (e2p if t else e2m)[...]
        w[pl.ds(t * 12 + 4, 4)] = own
        side = t - 1
        if 0 <= side < 10:
            w[pl.ds(t * 12, 4)] = zcm[4 * side : 4 * side + 4]
            w[pl.ds(t * 12 + 8, 4)] = zcp[4 * side : 4 * side + 4]

    def spot(t, z):
        return (t + 4) * 12 + z + 4

    row = 0
    for t, z, count in diamond(4):
        size = count * CP
        top, tail = halves(w[pl.ds(spot(t, z), count)].reshape(size, CC))
        packed[row : row + size, 0:CC] = top
        packed[row : row + size, CC : 2 * CC] = tail
        row += size
    both = dot(packed[...], csmat[...])
    first = both[:, 0:CC] + both[:, CC : 2 * CC]
    row = 0
    for t, z, count in diamond(4):
        size = count * CP
        value = first[row : row + size].reshape(count, CP, CC)
        w0[pl.ds(spot(t, z), count)] = value
        w[pl.ds(spot(t, z), count)] = value
        row += size
    turn = [coarse_ref[hop] for hop in range(4)]

    for sweep in range(SWEEPS):
        shape = diamond(SWEEPS - sweep)
        row = 0
        for t, z, count in shape:
            size = count * CP
            start = spot(t, z)
            blocks = [w[pl.ds(start + offset, count)].reshape(size, CC) for offset in (0, 12, -12, 1, -1)]
            for hop in range(4):
                blocks.append(
                    jnp.concatenate(
                        [jnp.take_along_axis(w[start + n], turn[hop], axis=0) for n in range(count)], axis=0
                    )
                )
            for hop, block in enumerate(blocks):
                top, tail = halves(block)
                operand[row : row + size, hop * CC : (hop + 1) * CC] = top
                operand[row : row + size, KC + hop * CC : KC + (hop + 1) * CC] = tail
            row += size
        both = dot(operand[0:row, :], cmat[...])
        change = both[:, 0:CC] + both[:, CC : 2 * CC]
        row = 0
        for t, z, count in shape:
            size = count * CP
            place_of = pl.ds(spot(t, z), count)
            w[place_of] = w[place_of] + w0[place_of] - change[row : row + size].reshape(count, CP, CC)
            row += size

    near = jnp.concatenate([w[pl.ds(spot(t, -1), 6)] for t in range(-1, 5)], axis=0)
    near = jnp.concatenate([near.reshape(36 * CP, CC), jnp.zeros((12 * CP, CC), F32)], axis=0)
    top, tail = halves(near)
    ptop, ptail = halves(prolong_ref[...])
    up = dot_nt(ptop, top) + dot_nt(ptop, tail) + dot_nt(ptail, top)
    for part in range(3):
        lifted[part] = up[:, part * PL : (part + 1) * PL]


def correct_kernel(
    lifted, lift_ref, plane_ref, x1, xm, xp, x0, lw, mmat,
    field, wide, first, last,
    vhigh, vlow,
):
    plane = plane_tables(plane_ref)
    home = jnp.broadcast_to(lift_ref[0:1, :], (CF, PL))

    def raised(t, z):
        number = (t + 1) * 6 + z + 1
        return lanes_of(lifted[lax.div(number, 16)], home + CP * lax.rem(number, 16))

    def correct(index, carry):
        t, z = lax.div(index, 3), 2 * lax.rem(index, 3) - 1
        for column in range(2):
            site = place(t, z) + column
            field[site] = x1[site] + raised(t, z + column)
        return carry

    lax.fori_loop(0, 12, correct, 0)

    def correct_outside(z, carry):
        field[place(-1, z)] = xm[z] + raised(-1, z)
        field[place(4, z)] = xp[z] + raised(4, z)
        return carry

    lax.fori_loop(0, 4, correct_outside, 0)

    def finish(t, half, changes):
        for column, change in enumerate(changes):
            site = place(t, 2 * half + column)
            new = field[site] + x0[site] - change
            wide[site] = new
            (last if t else first)[2 * half + column] = new

    block_pairs((0, 3), mmat, field, lw, plane, vhigh, vlow, finish)


def rest_kernel(
    field, wide_in, first, last, plane_ref, x0, lw, mmat,
    wide, second, third, zlow, zhigh,
    vhigh, vlow,
):
    plane = plane_tables(plane_ref)
    halves_in_z = (zlow, zhigh)
    for half, target in enumerate(halves_in_z):
        target[0:2] = first[2 * half : 2 * half + 2]
        target[6:8] = last[2 * half : 2 * half + 2]

    def finish(t, half, changes):
        for column, change in enumerate(changes):
            site = place(t, 2 * half + column)
            new = field[site] + x0[site] - change
            wide[site] = new
            (second if t == 1 else third)[2 * half + column] = new
            halves_in_z[half][2 * t + column] = new

    block_pairs((1, 2), mmat, field, lw, plane, vhigh, vlow, finish)


def inner_kernel(wide_in, hzm, hzp, x0, lw, mmat, plane_ref, wide, x4, vhigh, vlow):
    plane = plane_tables(plane_ref)
    for t in range(4):
        wide[pl.ds(place(t, -2), 2)] = hzm[2 * t : 2 * t + 2]
        wide[pl.ds(place(t, 4), 2)] = hzp[2 * t : 2 * t + 2]

    blank_rows(wide, -1, 6)
    sweeps(6, edge_pair, mmat, wide, x0, lw, plane, vhigh, vlow, x4)
    sweeps(6, middle_pair, mmat, wide, x0, lw, plane, vhigh, vlow, x4)


def post_kernel(
    wide_in, x4_in, tm1, tm2, tp1, tp2, czm, czp, a0, a1, a2, a3, x0, lw, mmat, bmat, mhops, plane_ref,
    wide, x4, sol_out, res_out,
    vhigh, vlow, rest, sems,
):
    plane = plane_tables(plane_ref)
    for source, t in ((tm1, -1), (tm2, -2), (tp1, 4), (tp2, 5)):
        wide[pl.ds(place(t, 0), 4)] = source[...]
    for source, z in ((czm, -1), (czp, 4)):
        wide[place(-1, z)] = source[0]
        wide[place(4, z)] = source[1]

    close_edges(mhops, wide, lw, vhigh, vlow, x4)
    sweeps(4, outer_pair, mmat, wide, x0, lw, plane, vhigh, vlow, x4)

    def send(source, target, number, kind):
        copy = pltpu.make_async_copy(source, target.at[:, number, :], sems.at[kind, number])
        copy.start()
        return copy

    copies = [send(x4.at[place(n // 4, n % 4)], sol_out, n, 0) for n in range(16)]
    rows = (a0, a1, a2, a3)

    def finish(t, half, images):
        for column, image in enumerate(images):
            number = 4 * t + 2 * half + column
            rest[number] = rows[t][2 * half + column, 0:CF, :] - image
            copies.append(send(rest.at[number], res_out, number, 1))

    block_pairs(range(4), bmat, x4, lw, plane, vhigh, vlow, finish)
    for copy in copies:
        copy.wait()


STACKED = ((2, 2, KF, PL), BF16)
FRAME = ((64, CF, PL), F32)
WEIGHTS = ((64, 8, PL), F32)
ROW = ((4, CF, PL), F32)
PAIRED = ((2 * CF, KF), BF16)


def call(kernel, outs, scratch, aliases, *args, limit=8, far=(), away=()):
    vmem, hbm = pl.BlockSpec(memory_space=pltpu.VMEM), pl.BlockSpec(memory_space=pltpu.HBM)
    built = pl.pallas_call(
        kernel,
        out_shape=tuple(jax.ShapeDtypeStruct(shape, kind) for shape, kind in outs),
        in_specs=[hbm if number in away else vmem for number in range(len(args))],
        out_specs=tuple(hbm if number in far else vmem for number in range(len(outs))),
        scratch_shapes=[
            pltpu.VMEM(*entry) if isinstance(entry, tuple) else entry for entry in scratch
        ],
        input_output_aliases=aliases,
        compiler_params=pltpu.CompilerParams(vmem_limit_bytes=limit << 20),
    )
    args = [
        pltpu.with_memory_space_constraint(value, pltpu.HBM) if number in away else value
        for number, value in enumerate(args)
    ]
    return built(*args)


def moved(value, axes, step):
    count = 1
    for axis in axes if isinstance(axes, tuple) else (axes,):
        count *= lax.axis_size(axis)
    return lax.ppermute(value, axes, [(i, (i + step) % count) for i in range(count)])


def shards(
    rhs_field,
    link_weights,
    fine_blocks,
    smoother,
    plane_next,
    aggregate,
    restrict_map,
    prolong_map,
    coarse_blocks,
    coarse_smoother,
    coarse_next,
):
    near = ((4, CF + 8, PL), F32)
    sides = ((8, CF + 8, PL), F32)
    lows, highs, *rows, links, s_near, blocks, restrict, plane, home = call(
        pack_kernel,
        (
            sides, sides, near, ROW, ROW, near, ((16, 8, PL), F32), ((CF, CF), F32), ((NB, CF, CF), F32),
            ((CF, CC), F32), ((4, PL), jnp.int32), ((1, PL), jnp.int32),
        ),
        (((CF * 16, PL), F32), ((8 * 16, PL), F32), pltpu.SemaphoreType.DMA((7,))),
        {},
        rhs_field.reshape(CF * 16, PL), link_weights.reshape(8 * 16, PL), smoother, fine_blocks,
        restrict_map, plane_next, aggregate.reshape(1, PL),
        away=range(7),
    )
    hzm, hzp = moved(highs, "gz", 1), moved(lows, "gz", -1)
    tm1, tp1 = moved(rows[3], TAXES, 1), moved(rows[0], TAXES, -1)
    ctm = moved(jnp.stack([hzm[7, 0:CF], hzp[6, 0:CF]]), TAXES, 1)
    ctp = moved(jnp.stack([hzm[1, 0:CF], hzp[0, 0:CF]]), TAXES, -1)

    hops = ((2, 2 * CF, CF), BF16)
    smat, mpair, bpair, mhops, bhops, member = call(
        prepare_kernel,
        (((2 * CF, CF), BF16), PAIRED, PAIRED, hops, hops, ((16, PL), F32)),
        (),
        {},
        s_near, blocks, home,
    )
    cpair, csmat, prolong = call(
        ready_kernel,
        (((2 * KC, 2 * CC), BF16), ((2 * CC, 2 * CC), BF16), ((CF, CC), F32)),
        (((CC, CC), F32), ((NB, CC, CC), F32), pltpu.SemaphoreType.DMA((3,))),
        {},
        coarse_smoother, coarse_blocks, prolong_map.T,
        away=range(3),
    )
    turn = jnp.broadcast_to(coarse_next[:, :, None], (4, CP, CC))

    x0, lw, x1 = call(
        local_kernel,
        (FRAME, WEIGHTS, FRAME),
        (STACKED, STACKED),
        {},
        *rows, links, hzm, hzp, smat, mpair, plane,
    )
    (x1,) = call(edge_kernel, (FRAME,), (STACKED, STACKED), {2: 0}, x0, lw, x1, mpair, plane)
    x0, lw, x1, up, down, first, last = call(
        pre_kernel,
        (FRAME, WEIGHTS, FRAME, ((20, CP, CC), F32), ((20, CP, CC), F32), ROW, ROW),
        (STACKED, STACKED, ((24 * CP, CF), F32)),
        {15: 0, 16: 1, 17: 2},
        *rows, tm1, tp1, ctm, ctp, smat, bpair, mhops, bhops, restrict, plane, member,
        x0, lw, x1,
    )

    tcm, tcp = moved(up, TAXES, 1), moved(down, TAXES, -1)
    e2m, e2p = moved(up[16:20], TAXES, 2), moved(down[16:20], TAXES, -2)
    whole, tall = call(
        join_kernel,
        (((48, CP, CC), F32), ((40, CP, CC), F32)),
        (),
        {},
        up, down, tcm, tcp,
    )
    zcm, zcp = moved(tall, "gz", 1), moved(tall, "gz", -1)
    xm, xp = moved(last, TAXES, 1), moved(first, TAXES, -1)

    (lifted,) = call(
        coarse_kernel,
        (((3, CF, PL), F32),),
        (
            ((144, CP, CC), F32),
            ((144, CP, CC), F32),
            ((104 * CP, 2 * CC), BF16),
            ((76 * CP, 2 * KC), BF16),
        ),
        {},
        whole, e2m, e2p, zcm, zcp, csmat, cpair, turn, prolong,
        limit=12,
    )
    field, wide, r0, r3 = call(
        correct_kernel,
        (FRAME, FRAME, ROW, ROW),
        (STACKED, STACKED),
        {},
        lifted, home, plane, x1, xm, xp, x0, lw, mpair,
    )
    half = ((8, CF, PL), F32)
    wide, r1, r2, low, high = call(
        rest_kernel,
        (FRAME, ROW, ROW, half, half),
        (STACKED, STACKED),
        {1: 0},
        field, wide, r0, r3, plane, x0, lw, mpair,
    )
    tm1, tp1 = moved(r3, TAXES, 1), moved(r0, TAXES, -1)
    tm2, tp2 = moved(r2, TAXES, 1), moved(r1, TAXES, -1)
    hzm, hzp = moved(high, "gz", 1), moved(low, "gz", -1)
    czm = moved(jnp.stack([tm1[3], tp1[3]]), "gz", 1)
    czp = moved(jnp.stack([tm1[0], tp1[0]]), "gz", -1)
    wide, x4 = call(
        inner_kernel,
        (FRAME, FRAME),
        (STACKED, STACKED),
        {0: 0},
        wide, hzm, hzp, x0, lw, mpair, plane,
    )
    _, _, sol, res = call(
        post_kernel,
        (FRAME, FRAME, ((CF, 16, PL), F32), ((CF, 16, PL), F32)),
        (STACKED, STACKED, ((16, CF, PL), F32), pltpu.SemaphoreType.DMA((2, 16))),
        {0: 0, 1: 1},
        wide, x4, tm1, tm2, tp1, tp2, czm, czp, *rows, x0, lw, mpair, bpair, mhops, plane,
        far=(2, 3),
    )

    def natural(value):
        return value.reshape(1, CF, 4, 4, PL)

    return natural(sol), natural(res)


def solution(mesh):
    spread = P(None, None, TAXES, "gz", None)
    return jax.shard_map(
        shards,
        mesh=mesh,
        in_specs=(spread, P(None, TAXES, "gz", None)) + (P(),) * 9,
        out_specs=(spread, spread),
        check_vma=False,
    )
```
